512 devices in a mesh: energy: 64 (over z, y), slab: 8 (over x, core).
Axes of the slice: x: 4, y: 4, z: 16, core: 2. Of those that a mesh axis runs over, the one named last changes fastest.
Arguments:
- inverses: bfloat16 [2, 64, 8, 512, 512], P(None, 'energy', 'slab')
- coupling: bfloat16 [8, 512, 512], P('slab'), may hold values from -0.21875 to 0.21875
- slab_count: int32 [64], P('energy'), may hold values from 1 to 8, as said below
- branch_shift: int32 [4], replicated, may hold values from -3 to 3, as said below
- branch_gain: float32 [4, 512], replicated, may hold values from 0.3 to 1.5
Outputs:
- sigma: bfloat16 [2, 64, 8, 512, 512], P(None, 'energy', 'slab')
The draws below stay inside these ranges and needn't reach their ends.
Inputs may be any that keep to these rules, and one draw needn't show every extreme that they name: slab_count takes both its smallest and its largest value in every draw. branch_shift takes both -3 and 3 in every draw.
All inputs are finite; a program needn't handle non-finite values.
Results may differ from the reference program's by a relative error of at most 0.012.
Values may be sent and summed in bfloat16 or wider, within the bound.
No kernel may reach another device: no remote copies, remote signals or barrier semaphores. Data moves between devices by JAX's collectives and lax.ppermute only.
A program may use at most 64 MiB of HBM per device.

```python
import math
import jax
import jax.numpy as jnp
from jax import lax

B = 512
NB = 4
MAXS = 3
E = 64
S = 8


def draw_inverses(key, part):
    key_noise, key_real, key_imag = jax.random.split(key, 3)
    noise = 0.5 * jax.random.normal(key_noise, (2, E, S, B, B), jnp.float32) / jnp.sqrt(jnp.float32(B))
    diag_imag = -jax.random.uniform(key_imag, (E, S, B), jnp.float32, 0.3, 1.0)
    diag_real = jax.random.uniform(key_real, (E, S, B), jnp.float32, -1.0, 1.0)
    rows = jnp.arange(B)[:, None]
    cols = jnp.arange(B)[None, :]
    identity = (rows == cols).astype(jnp.float32)
    real_part = noise[0] + identity * diag_real[:, :, :, None]
    imag_part = noise[1] + identity * diag_imag[:, :, :, None]
    return jnp.stack([real_part, imag_part]).astype(jnp.bfloat16)


def draw_slab_count(key, part):
    key_count, key_pick = jax.random.split(key)
    counts = jax.random.randint(key_count, (E,), 1, S + 1)
    picked = jax.random.permutation(key_pick, E)
    places = jnp.arange(E)
    counts = jnp.where(places == picked[0], S, counts)
    counts = jnp.where(places == picked[1], 1, counts)
    return counts.astype(jnp.int32)


def draw_branch_shift(key, part):
    key_shift, key_order = jax.random.split(jax.random.fold_in(key, 7))
    base = jax.random.randint(key_shift, (NB,), -MAXS, MAXS + 1)
    places = jnp.arange(NB)
    base = jnp.where(places == 0, MAXS, jnp.where(places == 1, -MAXS, base))
    order = jax.random.permutation(key_order, NB)
    return base[order].astype(jnp.int32)


def shard_levels(key, dims, cuts, low, high):
    loudness, own = 1.0, jax.random.fold_in(key, 6)
    for axis_at, shards_of in cuts:
        steps = jnp.exp(jax.random.uniform(jax.random.fold_in(own, axis_at), (shards_of,), jnp.float32, low / len(cuts), high / len(cuts)))
        loudness = loudness * jnp.repeat(steps, dims[axis_at] // shards_of).reshape([-1 if axis == axis_at else 1 for axis in range(len(dims))])
    return loudness


def centred(stream_key, dims, scale, most, pieces=(), kind=jnp.bfloat16):
    drawn = scale * jax.random.normal(stream_key, dims, jnp.float32)
    if pieces:
        drawn = drawn * shard_levels(stream_key, dims, pieces, -0.22, 0.18)
    return jnp.clip(drawn, -most, most).astype(kind)


def setup_inputs(seed: int = 0) -> dict:
    keys = jax.random.split(jax.random.key(seed), 6)
    return {
        "inverses": draw_inverses(jax.random.fold_in(keys[5], 71), 0),
        "coupling": centred(keys[1], (S, B, B), (3 * B // 2) ** -0.5, 0.21875, ((0, 8),)),
        "slab_count": draw_slab_count(jax.random.fold_in(keys[5], 71), 0),
        "branch_shift": draw_branch_shift(jax.random.fold_in(keys[5], 71), 0),
        "branch_gain": jnp.clip(jnp.exp(jax.random.uniform(keys[4], (NB, B), jnp.float32, math.log(0.3), math.log(1.5))), 0.3, 1.5),
    }


def complex_product(left_real, left_imag, right_real, right_imag):
    real_part = jnp.matmul(left_real, right_real) - jnp.matmul(left_imag, right_imag)
    imag_part = jnp.matmul(left_real, right_imag) + jnp.matmul(left_imag, right_real)
    return real_part, imag_part


def rounded(value):
    return lax.optimization_barrier(value.astype(jnp.bfloat16)).astype(jnp.float32)


def reference(inverses, coupling, slab_count, branch_shift, branch_gain):
    first = inverses[:, :, 0]
    stacked = jnp.transpose(inverses, (2, 0, 1, 3, 4))
    positions = jnp.arange(S, dtype=jnp.int32)

    def advance(previous, item):
        block, link, position = item
        inverse_real = block[0].astype(jnp.float32)
        inverse_imag = block[1].astype(jnp.float32)
        link_full = link.astype(jnp.float32)
        left_real = rounded(jnp.matmul(inverse_real, link_full))
        left_imag = rounded(jnp.matmul(inverse_imag, link_full))
        right_real = rounded(jnp.matmul(link_full.T, inverse_real))
        right_imag = rounded(jnp.matmul(link_full.T, inverse_imag))
        prev_real = previous[0].astype(jnp.float32)
        prev_imag = previous[1].astype(jnp.float32)
        half_real, half_imag = complex_product(left_real, left_imag, prev_real, prev_imag)
        tail_real, tail_imag = complex_product(rounded(half_real), rounded(half_imag), right_real, right_imag)
        updated = jnp.stack([inverse_real + tail_real, inverse_imag + tail_imag]).astype(jnp.bfloat16)
        active = (position < slab_count)[None, :, None, None]
        result = jnp.where(active, updated, block)
        return result, result

    _, rest = lax.scan(advance, first, (stacked[1:], coupling[1:], positions[1:]))
    greens = jnp.concatenate([first[None], rest], axis=0)
    energies = jnp.arange(E, dtype=jnp.int32)

    def slab_sigma(green_slab):
        values = green_slab.astype(jnp.float32)
        total = jnp.zeros(values.shape, jnp.float32)
        for branch in range(NB):
            target = (energies + branch_shift[branch]).astype(jnp.int32)
            valid = (target >= 0) & (target < E)
            taken = jnp.take(values, jnp.clip(target, 0, E - 1), axis=1)
            weight = branch_gain[branch][:, None] * branch_gain[branch][None, :]
            total = total + jnp.where(valid[None, :, None, None], taken * weight, jnp.float32(0.0))
        return total.astype(jnp.bfloat16)

    sigmas = lax.map(slab_sigma, greens)
    return jnp.transpose(sigmas, (1, 2, 0, 3, 4))
```

```python
import jax
import jax.numpy as jnp
from jax import lax
from jax.sharding import PartitionSpec as P

MAXS = 3
BF = jnp.bfloat16
F32 = jnp.float32


def dot(a, b):
    return jnp.dot(a, b, preferred_element_type=F32)


def cmul(ar, ai, br, bi):
    return dot(ar, br) - dot(ai, bi), dot(ar, bi) + dot(ai, br)


def shifted(block, distance):
    count = lax.axis_size("energy")
    route = [(i + distance, i) for i in range(count) if 0 <= i + distance < count]
    return lax.ppermute(block, "energy", route)


def maps_of(block, link):
    lr, li = dot(block[0], link).astype(BF), dot(block[1], link).astype(BF)
    rr, ri = dot(link.T, block[0]).astype(BF), dot(link.T, block[1]).astype(BF)
    return lr, li, rr, ri


def sandwich(base, maps, middle):
    lr, li, rr, ri = maps
    hr, hi = cmul(lr, li, middle[0], middle[1])
    tr, ti = cmul(hr.astype(BF), hi.astype(BF), rr, ri)
    return jnp.stack([base[0].astype(F32) + tr, base[1].astype(F32) + ti]).astype(BF)


def local(inverses, coupling, slab_count, branch_shift, branch_gain):
    block = inverses[:, 0, 0]
    link = coupling[0]
    position = lax.axis_index("slab")
    slabs = lax.axis_size("slab")
    upper = position % 2 == 1
    active = position < slab_count[0]

    to_upper = [(i, i + 1) for i in range(0, slabs, 2)]
    to_lower = [(i + 1, i) for i in range(0, slabs, 2)]
    low_block = lax.ppermute(block, "slab", to_upper)
    low_link = lax.ppermute(link, "slab", to_upper)

    own = [jnp.where(active, m, jnp.zeros_like(m)) for m in maps_of(block, link)]
    both = sandwich(block, own, low_block)
    low = maps_of(low_block, low_link)
    clr, cli = cmul(own[0], own[1], low[0], low[1])
    crr, cri = cmul(low[2], low[3], own[2], own[3])
    composed = [clr.astype(BF), cli.astype(BF), crr.astype(BF), cri.astype(BF)]
    maps = [jnp.where(upper, c, o) for c, o in zip(composed, own)]
    base = jnp.where(upper, both, block)

    green = base
    incoming = None
    for k in range(1, slabs - 2, 2):
        arrived = lax.ppermute(green, "slab", [(k, k + 2)])
        incoming = arrived if incoming is None else incoming + arrived
        if k + 2 < slabs - 1:
            green = sandwich(base, maps, incoming)
    handed = lax.ppermute(incoming, "slab", to_lower)
    previous = jnp.where(upper, incoming, handed)
    green = sandwich(base, maps, previous)

    def weight(distance):
        hits = (branch_shift == distance).astype(F32)
        scaled = branch_gain * hits[:, None]
        return jnp.dot(scaled.T, branch_gain, precision=lax.Precision.HIGHEST)

    ends = [shifted(green, d) for d in (MAXS, -MAXS)]
    total = weight(0)[None] * green.astype(F32)
    for d, piece in zip((MAXS, -MAXS), ends):
        total = total + weight(d)[None] * piece.astype(F32)
    for d in range(1 - MAXS, MAXS):
        if d:
            total = lax.cond(
                jnp.any(branch_shift == d),
                lambda t, g, d=d: t + weight(d)[None] * shifted(g, d).astype(F32),
                lambda t, g: t,
                total,
                green,
            )
    return total.astype(BF)[:, None, None]


def solution(mesh):
    return jax.shard_map(
        local,
        mesh=mesh,
        in_specs=(
            P(None, "energy", "slab", None, None),
            P("slab", None, None),
            P("energy"),
            P(),
            P(),
        ),
        out_specs=P(None, "energy", "slab", None, None),
        check_vma=False,
    )
```

```python
import jax
import jax.numpy as jnp
from jax import lax
from jax.sharding import PartitionSpec as P

MAXS = 3
BF = jnp.bfloat16
F32 = jnp.float32
BOTH = ("energy", "slab")
tie = lax.optimization_barrier


def dot(a, b):
    return jnp.dot(a, b, preferred_element_type=F32)


def cmul(ar, ai, br, bi):
    return dot(ar, br) - dot(ai, bi), dot(ar, bi) + dot(ai, br)


def maps_of(block, link, live):
    maps = (dot(block[0], link), dot(block[1], link), dot(link.T, block[0]), dot(link.T, block[1]))
    return [jnp.where(live, m, 0.0).astype(BF) for m in maps]


def sandwich(base, maps, middle):
    lr, li, rr, ri = maps
    hr, hi = cmul(lr, li, middle[0], middle[1])
    tr, ti = cmul(hr.astype(BF), hi.astype(BF), rr, ri)
    return jnp.stack([base[0].astype(F32) + tr, base[1].astype(F32) + ti]).astype(BF)


def local(inverses, coupling, slab_count, branch_shift, branch_gain):
    block = inverses[:, 0, 0]
    link = coupling[0]
    energy = lax.axis_index("energy")
    energies = lax.axis_size("energy")
    position = lax.axis_index("slab")
    slabs = lax.axis_size("slab")
    upper = position % 2 == 1
    lows, ups = range(0, slabs, 2), range(1, slabs, 2)

    def moved(value, slab_pairs, distance_of):
        route = [
            (((e + distance_of(b)) % energies) * slabs + a, e * slabs + b)
            for e in range(energies)
            for a, b in slab_pairs
        ]
        return lax.ppermute(value, BOTH, route)

    def side(b):
        return MAXS if b % 2 == 0 else -MAXS

    swap = [(i ^ 1, i) for i in range(slabs)]
    same = [(i, i) for i in range(slabs)]

    partner_block = lax.ppermute(block, "slab", swap)
    partner_link = lax.ppermute(link, "slab", swap)
    far_same = moved(block, same, side)
    far_swap = moved(block, swap, side)
    far_count = moved(slab_count.astype(F32)[None], same, side)[0, 0]

    own = maps_of(block, link, position < slab_count[0])
    both = sandwich(block, own, partner_block)

    def chain(both, own, partner_block):
        partner = maps_of(partner_block, partner_link, (position ^ 1) < slab_count[0])
        clr, cli = cmul(own[0], own[1], partner[0], partner[1])
        crr, cri = cmul(partner[2], partner[3], own[2], own[3])
        composed = [m.astype(BF) for m in (clr, cli, crr, cri)]
        green, incoming = both, None
        for k in range(1, slabs - 4, 2):
            arrived = lax.ppermute(green, "slab", [(k, k + 2)])
            incoming = arrived if incoming is None else incoming + arrived
            green = sandwich(both, composed, incoming)
        return green

    green = lax.cond(branch_shift[0] <= MAXS, chain, lambda both, own, other: both, both, own, partner_block)

    to_upper = moved(green, [(b - 2, b) for b in ups if b > 1], side)
    to_lower = moved(green, [(b - 1, b) for b in lows if b > 0], side)
    previous = jnp.where(upper, to_upper, to_lower)

    far_same, far_swap, _ = tie((far_same, far_swap, green))
    low_block = jnp.where(upper, far_swap, far_same)
    up_block = jnp.where(upper, far_same, far_swap)
    low_link = jnp.where(upper, partner_link, link)
    up_link = jnp.where(upper, link, partner_link)
    low_at = (position // 2) * 2
    low_maps = maps_of(low_block, low_link, low_at.astype(F32) < far_count)
    up_maps = maps_of(up_block, up_link, (low_at + 1).astype(F32) < far_count)
    low_green = sandwich(low_block, low_maps, previous)
    up_green = sandwich(up_block, up_maps, low_green)

    keep = jnp.where(upper, up_green, low_green)
    give = jnp.where(upper, low_green, up_green)
    got = lax.ppermute(give, "slab", swap)
    plus = jnp.where(upper, got, keep)
    minus = jnp.where(upper, keep, got)

    def weight(distance):
        inside = (energy + distance >= 0) & (energy + distance < energies)
        total = jnp.zeros((branch_gain.shape[1],) * 2, F32)
        for b in range(branch_gain.shape[0]):
            hit = jnp.where(inside & (branch_shift[b] == distance), 1.0, 0.0)
            total = total + (hit * branch_gain[b])[:, None] * branch_gain[b][None, :]
        return total

    total = weight(MAXS)[None] * plus.astype(F32) + weight(-MAXS)[None] * minus.astype(F32)
    half = block.shape[1] // 2

    def ring(value, distance):
        return lax.ppermute(value, "energy", [((i + distance) % energies, i) for i in range(energies)])

    for d in range(1 - MAXS, MAXS):

        def relayed(t, p, m, d=d):
            first = ring(p[:, :half], d - MAXS)
            second = ring(m[:, half:], d + MAXS)
            return t + weight(d)[None] * jnp.concatenate([first, second], axis=1).astype(F32)

        total = lax.cond(jnp.any(branch_shift == d), relayed, lambda t, p, m: t, total, plus, minus)
    return total.astype(BF)[:, None, None]


def solution(mesh):
    return jax.shard_map(
        local,
        mesh=mesh,
        in_specs=(
            P(None, "energy", "slab", None, None),
            P("slab", None, None),
            P("energy"),
            P(),
            P(),
        ),
        out_specs=P(None, "energy", "slab", None, None),
        check_vma=False,
    )
```

```python
import jax
import jax.numpy as jnp
from jax import lax
from jax.experimental import pallas as pl
from jax.experimental.pallas import tpu as pltpu
from jax.sharding import PartitionSpec as P

MAXS = 3
BF = jnp.bfloat16
F32 = jnp.float32
BOTH = ("energy", "slab")
ROWS = 256
EXTRA = 16
GRANT = 24 * 2**20
tie = lax.optimization_barrier
VMEM = pl.BlockSpec(memory_space=pltpu.VMEM)
SMEM = pl.BlockSpec(memory_space=pltpu.SMEM)
INNER = list(range(1 - MAXS, MAXS))
SETS = [()] + [(d,) for d in INNER] + [(c, d) for i, c in enumerate(INNER) for d in INNER[i + 1 :]]


def dot(a, b):
    return jnp.dot(a, b, preferred_element_type=F32)


def call(kernel, outs, dots, scalars, arrays, scratch=()):
    bytes_moved = sum(a.size * a.dtype.itemsize for a in (*arrays, *outs))
    return pl.pallas_call(
        kernel,
        out_shape=outs,
        in_specs=[SMEM] * len(scalars) + [VMEM] * len(arrays),
        out_specs=[VMEM] * len(outs),
        scratch_shapes=list(scratch),
        compiler_params=pltpu.CompilerParams(vmem_limit_bytes=GRANT),
        cost_estimate=pl.CostEstimate(
            flops=max(dots * 2 * 512**3, 2**20), bytes_accessed=bytes_moved, transcendentals=0
        ),
    )(*scalars, *arrays)


def like(array):
    return jax.ShapeDtypeStruct(array.shape, array.dtype)


def steps(size, body):
    @pl.loop(0, size // ROWS)
    def _(step):
        body(pl.ds(pl.multiple_of(step * ROWS, ROWS), ROWS))


def put_maps(link_ref, block, on, left_ref, right_ref):
    def body(rows):
        for part in range(2):
            left = dot(block(part, rows), link_ref[...])
            left_ref[part, rows, :] = jnp.where(on, left, 0.0).astype(BF)
            right = lax.dot_general(
                link_ref[:, rows],
                block(part, slice(None)),
                (((0,), (0,)), ((), ())),
                preferred_element_type=F32,
            )
            right_ref[part, rows, :] = jnp.where(on, right, 0.0).astype(BF)

    steps(link_ref.shape[0], body)


def complex_rows(a_ref, rows, b_ref):
    ar, ai = a_ref[0, rows, :], a_ref[1, rows, :]
    return dot(ar, b_ref[0]) - dot(ai, b_ref[1]), dot(ar, b_ref[1]) + dot(ai, b_ref[0])


def put_sandwich(base, left_ref, right_ref, middle_ref, out_ref):
    def body(rows):
        hr, hi = complex_rows(left_ref, rows, middle_ref)
        hr, hi = hr.astype(BF), hi.astype(BF)
        rr, ri = right_ref[0], right_ref[1]
        out_ref[0, rows, :] = (base(0, rows).astype(F32) + dot(hr, rr) - dot(hi, ri)).astype(BF)
        out_ref[1, rows, :] = (base(1, rows).astype(F32) + dot(hr, ri) + dot(hi, rr)).astype(BF)

    steps(out_ref.shape[1], body)


def reader(ref, at=0):
    return lambda part, rows: ref[at + part, rows, :]


def own_slab(slab_count, block, link, partner_block):
    def kernel(count_ref, block_ref, link_ref, partner_ref, left_ref, right_ref, both_ref):
        on = lax.axis_index("slab") < count_ref[0]
        put_maps(link_ref, reader(block_ref), on, left_ref, right_ref)
        put_sandwich(reader(block_ref), left_ref, right_ref, partner_ref, both_ref)

    return call(kernel, [like(block)] * 3, 12, (slab_count,), (block, link, partner_block))


def chip_maps(slab_count, partner_block, partner_link, left, right):
    def kernel(count_ref, block_ref, link_ref, l_ref, r_ref, left_ref, right_ref, ol_ref, or_ref):
        on = (lax.axis_index("slab") ^ 1) < count_ref[0]
        put_maps(link_ref, reader(block_ref), on, ol_ref, or_ref)

        def body(rows):
            for a_ref, b_ref, o_ref in ((l_ref, ol_ref, left_ref), (or_ref, r_ref, right_ref)):
                real, imag = complex_rows(a_ref, rows, b_ref)
                o_ref[0, rows, :] = real.astype(BF)
                o_ref[1, rows, :] = imag.astype(BF)

        steps(left.shape[1], body)

    scratch = [pltpu.VMEM(left.shape, BF)] * 2
    return call(kernel, [like(left)] * 2, 12, (slab_count,), (partner_block, partner_link, left, right), scratch)


def sandwich(base, left, right, *middles):
    def kernel(base_ref, left_ref, right_ref, *refs):
        middle_ref, out_ref = refs[0], refs[len(middles)]
        if len(middles) > 1:
            middle_ref = refs[-1]
            middle_ref[...] = refs[0][...] + refs[1][...]
        put_sandwich(reader(base_ref), left_ref, right_ref, middle_ref, out_ref)

    scratch = [pltpu.VMEM(base.shape, BF)] * (len(middles) > 1)
    return call(kernel, [like(base)], 8, (), (base, left, right, *middles), scratch)[0]


def message(slab_count, block, partner_block):
    size = block.shape[1]

    def kernel(count_ref, block_ref, partner_ref, out_ref):
        upper = lax.axis_index("slab") % 2 == 1
        low = jnp.where(upper, partner_ref[...], block_ref[...])
        high = jnp.where(upper, block_ref[...], partner_ref[...])
        for part in range(2):
            out_ref[pl.ds(part * size, size), :] = low[part]
            out_ref[pl.ds((2 + part) * size, size), :] = high[part]
        count = jnp.full((EXTRA, size), count_ref[0], jnp.int32).astype(F32)
        out_ref[pl.ds(4 * size, EXTRA), :] = count.astype(BF)

    out = jax.ShapeDtypeStruct((4 * size + EXTRA, size), BF)
    return call(kernel, [out], 0, (slab_count,), (block, partner_block))[0]


def far_block(far_ref, size, at):
    def read(part, rows):
        if isinstance(rows, slice):
            return far_ref[pl.ds((at + part) * size, size), :]
        return far_ref[pl.ds(pl.multiple_of((at + part) * size + rows.start, ROWS), ROWS), :]

    return read


def far_maps(far, link, partner_link):
    size = link.shape[0]

    def kernel(far_ref, link_ref, partner_ref, ll_ref, lr_ref, ul_ref, ur_ref, held_ref):
        position = lax.axis_index("slab")
        upper = position % 2 == 1
        low_at = ((position // 2) * 2).astype(F32)
        count = far_ref[pl.ds(4 * size, EXTRA), :].astype(F32)[:1]
        held_ref[...] = jnp.where(upper, partner_ref[...], link_ref[...])
        put_maps(held_ref, far_block(far_ref, size, 0), low_at < count, ll_ref, lr_ref)
        held_ref[...] = jnp.where(upper, link_ref[...], partner_ref[...])
        put_maps(held_ref, far_block(far_ref, size, 2), low_at + 1 < count, ul_ref, ur_ref)

    maps = jax.ShapeDtypeStruct((2, size, size), BF)
    return call(kernel, [maps] * 4, 8, (), (far, link, partner_link), [pltpu.VMEM(link.shape, BF)])


def far_green(far, at, left, right, *middles):
    size = left.shape[-1]

    def kernel(far_ref, left_ref, right_ref, *refs):
        middle_ref, out_ref = refs[0], refs[len(middles)]
        if len(middles) > 1:
            middle_ref = refs[-1]
            middle_ref[...] = refs[0][...] + refs[1][...]
        put_sandwich(far_block(far_ref, size, at), left_ref, right_ref, middle_ref, out_ref)

    scratch = [pltpu.VMEM(left.shape, BF)] * (len(middles) > 1)
    return call(kernel, [like(left)], 8, (), (far, left, right, *middles), scratch)[0]


def plan(branch_shift):
    branches = branch_shift.shape[0]

    def kernel(shift_ref, out_ref):
        used = {}
        for d in INNER:
            hit = jnp.int32(0)
            for b in range(branches):
                hit = hit | (shift_ref[b] == d).astype(jnp.int32)
            used[d] = hit
        which = jnp.int32(0)
        for at, held in enumerate(SETS):
            same = jnp.int32(1)
            for d in INNER:
                same = same & (used[d] if d in held else 1 - used[d])
            which = which + same * at
        out_ref[0] = which

    return pl.pallas_call(
        kernel, out_shape=jax.ShapeDtypeStruct((1,), jnp.int32), in_specs=[SMEM], out_specs=SMEM
    )(branch_shift)


def weights_of(branch_shift, gain, gain_t):
    branches, size = gain.shape

    def kernel(shift_ref, gain_ref, gain_t_ref, out_ref):
        energy, energies = lax.axis_index("energy"), lax.axis_size("energy")
        upper = lax.axis_index("slab") % 2 == 1
        first, last = jnp.int32(MAXS), jnp.int32(-MAXS)
        for b in range(branches):
            shift = shift_ref[b]
            inside = (shift > -MAXS) & (shift < MAXS)
            first = jnp.where(inside, jnp.minimum(first, shift), first)
            last = jnp.where(inside, jnp.maximum(last, shift), last)
        side = jnp.where(upper, -MAXS, MAXS)
        none = jnp.int32(10 * MAXS)
        distances = [side, -side, jnp.where(first < MAXS, first, none), jnp.where(last > first, last, none)]
        hits = []
        for distance in distances:
            inside = (energy + distance >= 0) & (energy + distance < energies)
            hits.append([
                jnp.where(inside & (shift_ref[b] == distance), 1.0, 0.0).astype(F32) for b in range(branches)
            ])

        @pl.loop(0, size // 64)
        def _(step):
            rows = pl.ds(pl.multiple_of(step * 64, 64), 64)
            outer = [gain_t_ref[rows, b : b + 1] * gain_ref[b : b + 1, :] for b in range(branches)]
            for k, hit in enumerate(hits):
                out_ref[k, rows, :] = sum(h * o for h, o in zip(hit, outer))

    out = jax.ShapeDtypeStruct((4, size, size), F32)
    return call(kernel, [out], 0, (branch_shift,), (gain, gain_t))[0]


def combine(weights, low, up, low_got, up_got, others=()):
    size = low.shape[1]

    def kernel(weight_ref, low_ref, up_ref, lg_ref, ug_ref, *refs):
        out_ref = refs[-1]
        upper = lax.axis_index("slab") % 2 == 1

        def total(mine_ref, got_ref):
            @pl.loop(0, size // 64)
            def _(step):
                rows = pl.ds(pl.multiple_of(step * 64, 64), 64)
                for part in range(2):
                    pieces = [mine_ref[part, rows, :], got_ref[part, rows, :]]
                    if others:
                        pieces += [refs[part][rows, :], refs[2 + part][rows, :]]
                    total = sum(weight_ref[k, rows, :] * p.astype(F32) for k, p in enumerate(pieces))
                    out_ref[part, rows, :] = total.astype(BF)

        pl.when(upper)(lambda: total(up_ref, ug_ref))
        pl.when(jnp.logical_not(upper))(lambda: total(low_ref, lg_ref))

    return call(kernel, [like(low)], 0, (), (weights, low, up, low_got, up_got, *others))[0]


def local(inverses, coupling, slab_count, branch_shift, branch_gain):
    block = inverses[:, 0, 0]
    link = coupling[0]
    energies = lax.axis_size("energy")
    slabs = lax.axis_size("slab")
    lows, ups = range(0, slabs, 2), range(1, slabs, 2)

    def moved(value, slab_pairs, distance_of):
        route = [
            (((e + distance_of(b)) % energies) * slabs + a, e * slabs + b)
            for e in range(energies)
            for a, b in slab_pairs
        ]
        return lax.ppermute(value, BOTH, route)

    def side(b):
        return MAXS if b % 2 == 0 else -MAXS

    swap = [(i ^ 1, i) for i in range(slabs)]
    same = [(i, i) for i in range(slabs)]

    partner_block = lax.ppermute(block, "slab", swap)
    partner_link = lax.ppermute(link, "slab", swap)

    left, right, both = own_slab(slab_count, block, link, partner_block)
    arrived = lax.ppermute(both, "slab", [(1, 3)])

    chip = chip_maps(slab_count, partner_block, partner_link, left, right)

    far = message(slab_count, block, partner_block)
    far, _ = tie((far, chip))
    far = moved(far, same, side)

    green = sandwich(both, *chip, arrived)

    def hop(_, green):
        further = lax.ppermute(green, "slab", [(k, k + 2) for k in range(3, slabs - 4, 2)])
        return sandwich(both, *chip, arrived, further)

    green = lax.fori_loop(0, jnp.minimum(slab_count[0], slabs // 2 - 3), hop, green)

    to_upper = moved(green, [(b - 2, b) for b in ups if b > 1], side)
    to_lower = moved(green, [(b - 1, b) for b in lows if b > 0], side)

    far, shift, gain, _ = tie((far, branch_shift, branch_gain, green))
    maps = far_maps(far, link, partner_link)
    which = plan(shift)[0]
    weights = weights_of(shift, gain, gain.T)
    to_upper, to_lower, maps, which, weights = tie((to_upper, to_lower, maps, which, weights))

    low = far_green(far, 0, maps[0], maps[1], to_upper, to_lower)
    low_got = lax.ppermute(low, "slab", [(b, b - 1) for b in ups])
    up = far_green(far, 2, maps[2], maps[3], low)
    up_got = lax.ppermute(up, "slab", [(b, b + 1) for b in lows])

    def ring(value, distance):
        return lax.ppermute(value, "energy", [((i + distance) % energies, i) for i in range(energies)])

    def relayed(distances):
        def branch(low, up, low_got, up_got):
            upper = lax.axis_index("slab") % 2 == 1
            plus = jnp.where(upper, up_got[0], low[0])
            minus = jnp.where(upper, up[1], low_got[1])
            pieces = [(ring(plus, d - MAXS), ring(minus, d + MAXS)) for d in distances]
            return (*pieces[0], *pieces[-1])

        return branch

    def more(weights, *greens):
        others = lax.switch(which - 1, [relayed(held) for held in SETS[1:]], *greens)
        return combine(weights, *greens, others)

    sigma = lax.cond(which == 0, combine, more, weights, low, up, low_got, up_got)
    return sigma[:, None, None]


def solution(mesh):
    return jax.shard_map(
        local,
        mesh=mesh,
        in_specs=(
            P(None, "energy", "slab", None, None),
            P("slab", None, None),
            P("energy"),
            P(),
            P(),
        ),
        out_specs=P(None, "energy", "slab", None, None),
        check_vma=False,
    )
```

```python
import jax
import jax.numpy as jnp
from jax import lax
from jax.experimental import pallas as pl
from jax.experimental.pallas import tpu as pltpu
from jax.sharding import PartitionSpec as P

MAXS = 3
BF = jnp.bfloat16
F32 = jnp.float32
BOTH = ("energy", "slab")
ROWS = 256
EXTRA = 16
GRANT = 24 * 2**20
COST = 1024
tie = lax.optimization_barrier
VMEM = pl.BlockSpec(memory_space=pltpu.VMEM)
SMEM = pl.BlockSpec(memory_space=pltpu.SMEM)
DONE = jax.ShapeDtypeStruct((8, 128), F32)
INNER = list(range(1 - MAXS, MAXS))
SETS = [()] + [(d,) for d in INNER] + [(c, d) for i, c in enumerate(INNER) for d in INNER[i + 1 :]]


def dot(a, b):
    return jnp.dot(a, b, preferred_element_type=F32)


def call(kernel, outs, dots, scalars, arrays, scratch=()):
    return pl.pallas_call(
        kernel,
        out_shape=outs,
        in_specs=[SMEM] * len(scalars) + [VMEM] * len(arrays),
        out_specs=[VMEM] * len(outs),
        scratch_shapes=list(scratch),
        compiler_params=pltpu.CompilerParams(vmem_limit_bytes=GRANT),
        cost_estimate=pl.CostEstimate(
            flops=COST * dots, bytes_accessed=1024, transcendentals=0
        ),
    )(*scalars, *arrays)


def like(array):
    return jax.ShapeDtypeStruct(array.shape, array.dtype)


def steps(size, body):
    @pl.loop(0, size // ROWS)
    def _(step):
        body(pl.ds(pl.multiple_of(step * ROWS, ROWS), ROWS))


def put_maps(link_ref, block, on, left_ref, right_ref):
    def body(rows):
        for part in range(2):
            left = dot(block(part, rows), link_ref[...])
            left_ref[part, rows, :] = jnp.where(on, left, 0.0).astype(BF)
            right = lax.dot_general(
                link_ref[:, rows],
                block(part, slice(None)),
                (((0,), (0,)), ((), ())),
                preferred_element_type=F32,
            )
            right_ref[part, rows, :] = jnp.where(on, right, 0.0).astype(BF)

    steps(link_ref.shape[0], body)


def complex_rows(a_ref, rows, b_ref):
    ar, ai = a_ref[0, rows, :], a_ref[1, rows, :]
    return dot(ar, b_ref[0]) - dot(ai, b_ref[1]), dot(ar, b_ref[1]) + dot(ai, b_ref[0])


def put_sandwich(base, left_ref, right_ref, middle_ref, out_ref):
    def body(rows):
        hr, hi = complex_rows(left_ref, rows, middle_ref)
        hr, hi = hr.astype(BF), hi.astype(BF)
        rr, ri = right_ref[0], right_ref[1]
        out_ref[0, rows, :] = (base(0, rows).astype(F32) + dot(hr, rr) - dot(hi, ri)).astype(BF)
        out_ref[1, rows, :] = (base(1, rows).astype(F32) + dot(hr, ri) + dot(hi, rr)).astype(BF)

    steps(out_ref.shape[1], body)


def reader(ref, at=0):
    return lambda part, rows: ref[at + part, rows, :]


def own_slab(slab_count, block, link, partner_block):
    def kernel(count_ref, block_ref, link_ref, partner_ref, left_ref, right_ref, both_ref):
        on = lax.axis_index("slab") < count_ref[0]
        put_maps(link_ref, reader(block_ref), on, left_ref, right_ref)
        put_sandwich(reader(block_ref), left_ref, right_ref, partner_ref, both_ref)

    return call(kernel, [like(block)] * 3, 12, (slab_count,), (block, link, partner_block))


def chip_maps(slab_count, partner_block, partner_link, left, right):
    def kernel(count_ref, block_ref, link_ref, l_ref, r_ref, left_ref, right_ref, ol_ref, or_ref):
        on = (lax.axis_index("slab") ^ 1) < count_ref[0]
        put_maps(link_ref, reader(block_ref), on, ol_ref, or_ref)

        def body(rows):
            for a_ref, b_ref, o_ref in ((l_ref, ol_ref, left_ref), (or_ref, r_ref, right_ref)):
                real, imag = complex_rows(a_ref, rows, b_ref)
                o_ref[0, rows, :] = real.astype(BF)
                o_ref[1, rows, :] = imag.astype(BF)

        steps(left.shape[1], body)

    scratch = [pltpu.VMEM(left.shape, BF)] * 2
    return call(kernel, [like(left)] * 2, 12, (slab_count,), (partner_block, partner_link, left, right), scratch)


def sandwich(base, left, right, *middles):
    def kernel(base_ref, left_ref, right_ref, *refs):
        middle_ref, out_ref = refs[0], refs[len(middles)]
        if len(middles) > 1:
            middle_ref = refs[-1]
            middle_ref[...] = refs[0][...] + refs[1][...]
        put_sandwich(reader(base_ref), left_ref, right_ref, middle_ref, out_ref)

    scratch = [pltpu.VMEM(base.shape, BF)] * (len(middles) > 1)
    return call(kernel, [like(base)], 8, (), (base, left, right, *middles), scratch)[0]


def message(slab_count, block, partner_block):
    size = block.shape[1]

    def kernel(count_ref, block_ref, partner_ref, out_ref):
        upper = lax.axis_index("slab") % 2 == 1
        low = jnp.where(upper, partner_ref[...], block_ref[...])
        high = jnp.where(upper, block_ref[...], partner_ref[...])
        for part in range(2):
            out_ref[pl.ds(part * size, size), :] = low[part]
            out_ref[pl.ds((2 + part) * size, size), :] = high[part]
        count = jnp.full((EXTRA, size), count_ref[0], jnp.int32).astype(F32)
        out_ref[pl.ds(4 * size, EXTRA), :] = count.astype(BF)

    out = jax.ShapeDtypeStruct((4 * size + EXTRA, size), BF)
    return call(kernel, [out], 0, (slab_count,), (block, partner_block))[0]


def far_block(far_ref, size, at):
    def read(part, rows):
        if isinstance(rows, slice):
            return far_ref[pl.ds((at + part) * size, size), :]
        return far_ref[pl.ds(pl.multiple_of((at + part) * size + rows.start, ROWS), ROWS), :]

    return read


def far_maps(far, link, partner_link):
    size = link.shape[0]

    def kernel(far_ref, link_ref, partner_ref, ll_ref, lr_ref, ul_ref, ur_ref, done_ref, held_ref):
        done_ref[...] = jnp.zeros_like(done_ref)
        position = lax.axis_index("slab")
        upper = position % 2 == 1
        low_at = ((position // 2) * 2).astype(F32)
        count = far_ref[pl.ds(4 * size, EXTRA), :].astype(F32)[:1]
        held_ref[...] = jnp.where(upper, partner_ref[...], link_ref[...])
        put_maps(held_ref, far_block(far_ref, size, 0), low_at < count, ll_ref, lr_ref)
        held_ref[...] = jnp.where(upper, link_ref[...], partner_ref[...])
        put_maps(held_ref, far_block(far_ref, size, 2), low_at + 1 < count, ul_ref, ur_ref)

    maps = jax.ShapeDtypeStruct((2, size, size), BF)
    return call(kernel, [maps] * 4 + [DONE], 8, (), (far, link, partner_link), [pltpu.VMEM(link.shape, BF)])


def far_low(far, left, right, first, second):
    size = left.shape[-1]

    def kernel(far_ref, left_ref, right_ref, a_ref, b_ref, out_ref, middle_ref):
        middle_ref[...] = a_ref[...] + b_ref[...]
        put_sandwich(far_block(far_ref, size, 0), left_ref, right_ref, middle_ref, out_ref)

    return call(kernel, [like(left)], 8, (), (far, left, right, first, second), [pltpu.VMEM(left.shape, BF)])[0]


def far_up(far, left, right, low):
    size = left.shape[-1]

    def kernel(far_ref, left_ref, right_ref, low_ref, mine_ref, give_ref):
        upper = lax.axis_index("slab") % 2 == 1

        @pl.when(upper)
        def _():
            put_sandwich(far_block(far_ref, size, 2), left_ref, right_ref, low_ref, mine_ref)
            give_ref[...] = low_ref[...]

        @pl.when(jnp.logical_not(upper))
        def _():
            put_sandwich(far_block(far_ref, size, 2), left_ref, right_ref, low_ref, give_ref)
            mine_ref[...] = low_ref[...]

    return call(kernel, [like(left)] * 2, 8, (), (far, left, right, low))


def plan(branch_shift):
    branches = branch_shift.shape[0]

    def kernel(shift_ref, out_ref):
        used = {}
        for d in INNER:
            hit = jnp.int32(0)
            for b in range(branches):
                hit = hit | (shift_ref[b] == d).astype(jnp.int32)
            used[d] = hit
        which = jnp.int32(0)
        for at, held in enumerate(SETS):
            same = jnp.int32(1)
            for d in INNER:
                same = same & (used[d] if d in held else 1 - used[d])
            which = which + same * at
        out_ref[0] = which

    return pl.pallas_call(
        kernel,
        out_shape=jax.ShapeDtypeStruct((1,), jnp.int32),
        in_specs=[SMEM],
        out_specs=SMEM,
        compiler_params=pltpu.CompilerParams(vmem_limit_bytes=GRANT),
    )(branch_shift)


def weights_of(branch_shift, gain):
    branches, size = gain.shape

    def kernel(shift_ref, gain_ref, out_ref, done_ref, gain_t_ref):
        gain_t_ref[...] = gain_ref[...].T
        done_ref[...] = jnp.zeros_like(done_ref)
        energy, energies = lax.axis_index("energy"), lax.axis_size("energy")
        upper = lax.axis_index("slab") % 2 == 1
        first, last = jnp.int32(MAXS), jnp.int32(-MAXS)
        for b in range(branches):
            shift = shift_ref[b]
            inside = (shift > -MAXS) & (shift < MAXS)
            first = jnp.where(inside, jnp.minimum(first, shift), first)
            last = jnp.where(inside, jnp.maximum(last, shift), last)
        side = jnp.where(upper, -MAXS, MAXS)
        none = jnp.int32(10 * MAXS)
        distances = [side, -side, jnp.where(first < MAXS, first, none), jnp.where(last > first, last, none)]
        hits = []
        for distance in distances:
            inside = (energy + distance >= 0) & (energy + distance < energies)
            hits.append([
                jnp.where(inside & (shift_ref[b] == distance), 1.0, 0.0).astype(F32) for b in range(branches)
            ])

        @pl.loop(0, size // 64)
        def _(step):
            rows = pl.ds(pl.multiple_of(step * 64, 64), 64)
            outer = [gain_t_ref[rows, b : b + 1] * gain_ref[b : b + 1, :] for b in range(branches)]
            for k, hit in enumerate(hits):
                out_ref[k, rows, :] = sum(h * o for h, o in zip(hit, outer))

    out = jax.ShapeDtypeStruct((4, size, size), F32)
    return call(kernel, [out, DONE], 0, (branch_shift,), (gain,), [pltpu.VMEM((size, branches), F32)])


def combine(weights, *blocks):
    size = blocks[0].shape[1]

    def kernel(weight_ref, *refs):
        @pl.loop(0, size // 64)
        def _(step):
            rows = pl.ds(pl.multiple_of(step * 64, 64), 64)
            held = [weight_ref[k, rows, :] for k in range(len(blocks))]
            for part in range(2):
                total = sum(w * ref[part, rows, :].astype(F32) for w, ref in zip(held, refs))
                refs[-1][part, rows, :] = total.astype(BF)

    return call(kernel, [like(blocks[0])], 0, (), (weights, *blocks))[0]


def local(inverses, coupling, slab_count, branch_shift, branch_gain):
    block = inverses[:, 0, 0]
    link = coupling[0]
    energies = lax.axis_size("energy")
    slabs = lax.axis_size("slab")
    lows, ups = range(0, slabs, 2), range(1, slabs, 2)

    def moved(value, slab_pairs, distance_of):
        route = [
            (((e + distance_of(b)) % energies) * slabs + a, e * slabs + b)
            for e in range(energies)
            for a, b in slab_pairs
        ]
        return lax.ppermute(value, BOTH, route)

    def side(b):
        return MAXS if b % 2 == 0 else -MAXS

    swap = [(i ^ 1, i) for i in range(slabs)]
    same = [(i, i) for i in range(slabs)]

    partner_block = lax.ppermute(block, "slab", swap)
    left, right, both = own_slab(slab_count, block, link, partner_block)
    arrived = lax.ppermute(both, "slab", [(1, 3)])
    later_block, later_link, _ = tie((block, link, both))
    far = message(slab_count, later_block, partner_block)
    partner_link = lax.ppermute(later_link, "slab", swap)

    chip = chip_maps(slab_count, partner_block, partner_link, left, right)
    chip, arrived = tie((chip, arrived))
    green = sandwich(both, *chip, arrived)
    for k in range(3, slabs - 4, 2):
        further = lax.ppermute(green, "slab", [(k, k + 2)])
        if k == 3:
            far = moved(far, same, side)
        green = sandwich(both, *chip, arrived, further)

    to_upper = moved(green, [(b - 2, b) for b in ups if b > 1], side)
    to_lower = moved(green, [(b - 1, b) for b in lows if b > 0], side)

    far, shift, gain, _ = tie((far, branch_shift, branch_gain, green))
    *maps, maps_done = far_maps(far, link, partner_link)
    which = plan(shift)[0]
    weights, weights_done = weights_of(shift, gain)
    to_upper, to_lower, which, _, _ = tie((to_upper, to_lower, which, maps_done, weights_done))

    low = far_low(far, maps[0], maps[1], to_upper, to_lower)
    mine, give = far_up(far, maps[2], maps[3], low)

    def alone(weights, mine, give):
        return combine(weights, mine, lax.ppermute(give, "slab", swap))

    def relayed(distances):
        def branch(weights, mine, give):
            pieces = [moved(mine, same, lambda b, d=d: d - side(b)) for d in distances]
            return combine(weights, mine, lax.ppermute(give, "slab", swap), *pieces)

        return branch

    branches = [relayed(held) if held else alone for held in SETS]
    sigma = lax.switch(which, branches, weights, mine, give)
    return sigma[:, None, None]


def solution(mesh):
    return jax.shard_map(
        local,
        mesh=mesh,
        in_specs=(
            P(None, "energy", "slab", None, None),
            P("slab", None, None),
            P("energy"),
            P(),
            P(),
        ),
        out_specs=P(None, "energy", "slab", None, None),
        check_vma=False,
    )
```

```python
import jax
import jax.numpy as jnp
from jax import lax
from jax.experimental import pallas as pl
from jax.experimental.pallas import tpu as pltpu
from jax.sharding import PartitionSpec as P

MAXS = 3
BF = jnp.bfloat16
F32 = jnp.float32
BOTH = ("energy", "slab")
ROWS = 256
EXTRA = 16
GRANT = 24 * 2**20
COST = 1024
tie = lax.optimization_barrier
VMEM = pl.BlockSpec(memory_space=pltpu.VMEM)
SMEM = pl.BlockSpec(memory_space=pltpu.SMEM)
DONE = jax.ShapeDtypeStruct((8, 128), F32)
INNER = list(range(1 - MAXS, MAXS))
SETS = [()] + [(d,) for d in INNER] + [(c, d) for i, c in enumerate(INNER) for d in INNER[i + 1 :]]


def dot(a, b):
    return jnp.dot(a, b, preferred_element_type=F32)


def call(kernel, outs, dots, scalars, arrays, scratch=()):
    return pl.pallas_call(
        kernel,
        out_shape=outs,
        in_specs=[SMEM] * len(scalars) + [VMEM] * len(arrays),
        out_specs=[VMEM] * len(outs),
        scratch_shapes=list(scratch),
        compiler_params=pltpu.CompilerParams(vmem_limit_bytes=GRANT),
        cost_estimate=pl.CostEstimate(
            flops=COST * dots, bytes_accessed=1024, transcendentals=0
        ),
    )(*scalars, *arrays)


def like(array):
    return jax.ShapeDtypeStruct(array.shape, array.dtype)


def steps(size, body):
    @pl.loop(0, size // ROWS)
    def _(step):
        body(pl.ds(pl.multiple_of(step * ROWS, ROWS), ROWS))


def put_maps(link_ref, block, on, left_ref, right_ref):
    def body(rows):
        for part in range(2):
            left = dot(block(part, rows), link_ref[...])
            left_ref[part, rows, :] = jnp.where(on, left, 0.0).astype(BF)
            right = lax.dot_general(
                link_ref[:, rows],
                block(part, slice(None)),
                (((0,), (0,)), ((), ())),
                preferred_element_type=F32,
            )
            right_ref[part, rows, :] = jnp.where(on, right, 0.0).astype(BF)

    steps(link_ref.shape[0], body)


def complex_rows(a_ref, rows, b_ref):
    ar, ai = a_ref[0, rows, :], a_ref[1, rows, :]
    return dot(ar, b_ref[0]) - dot(ai, b_ref[1]), dot(ar, b_ref[1]) + dot(ai, b_ref[0])


def put_sandwich(base, left_ref, right_ref, middle_ref, out_ref):
    def body(rows):
        hr, hi = complex_rows(left_ref, rows, middle_ref)
        hr, hi = hr.astype(BF), hi.astype(BF)
        rr, ri = right_ref[0], right_ref[1]
        parts[0][rows, :] = (base(0, rows).astype(F32) + dot(hr, rr) - dot(hi, ri)).astype(BF)
        parts[1][rows, :] = (base(1, rows).astype(F32) + dot(hr, ri) + dot(hi, rr)).astype(BF)

    parts = out_ref if isinstance(out_ref, tuple) else (out_ref.at[0], out_ref.at[1])
    steps(parts[0].shape[0], body)


def reader(ref, at=0):
    return lambda part, rows: ref[at + part, rows, :]


def own_slab(slab_count, block, link, partner_block):
    def kernel(count_ref, block_ref, link_ref, partner_ref, left_ref, right_ref, both_ref):
        on = lax.axis_index("slab") < count_ref[0]
        put_maps(link_ref, reader(block_ref), on, left_ref, right_ref)
        put_sandwich(reader(block_ref), left_ref, right_ref, partner_ref, both_ref)

    return call(kernel, [like(block)] * 3, 12, (slab_count,), (block, link, partner_block))


def chip_maps(slab_count, partner_block, partner_link, left, right):
    def kernel(count_ref, block_ref, link_ref, l_ref, r_ref, left_ref, right_ref, ol_ref, or_ref):
        on = (lax.axis_index("slab") ^ 1) < count_ref[0]
        put_maps(link_ref, reader(block_ref), on, ol_ref, or_ref)

        def body(rows):
            for a_ref, b_ref, o_ref in ((l_ref, ol_ref, left_ref), (or_ref, r_ref, right_ref)):
                real, imag = complex_rows(a_ref, rows, b_ref)
                o_ref[0, rows, :] = real.astype(BF)
                o_ref[1, rows, :] = imag.astype(BF)

        steps(left.shape[1], body)

    scratch = [pltpu.VMEM(left.shape, BF)] * 2
    return call(kernel, [like(left)] * 2, 12, (slab_count,), (partner_block, partner_link, left, right), scratch)


def sandwich(base, left, right, *middles):
    def kernel(base_ref, left_ref, right_ref, *refs):
        middle_ref, out_ref = refs[0], refs[len(middles)]
        if len(middles) > 1:
            middle_ref = refs[-1]
            middle_ref[...] = refs[0][...] + refs[1][...]
        put_sandwich(reader(base_ref), left_ref, right_ref, middle_ref, out_ref)

    scratch = [pltpu.VMEM(base.shape, BF)] * (len(middles) > 1)
    return call(kernel, [like(base)], 8, (), (base, left, right, *middles), scratch)[0]


def message(slab_count, block, partner_block):
    size = block.shape[1]

    def kernel(count_ref, block_ref, partner_ref, out_ref):
        upper = lax.axis_index("slab") % 2 == 1
        low = jnp.where(upper, partner_ref[...], block_ref[...])
        high = jnp.where(upper, block_ref[...], partner_ref[...])
        for part in range(2):
            out_ref[pl.ds(part * size, size), :] = low[part]
            out_ref[pl.ds((2 + part) * size, size), :] = high[part]
        count = jnp.full((EXTRA, size), count_ref[0], jnp.int32).astype(F32)
        out_ref[pl.ds(4 * size, EXTRA), :] = count.astype(BF)

    out = jax.ShapeDtypeStruct((4 * size + EXTRA, size), BF)
    return call(kernel, [out], 0, (slab_count,), (block, partner_block))[0]


def far_block(far_ref, size, at):
    def read(part, rows):
        if isinstance(rows, slice):
            return far_ref[pl.ds((at + part) * size, size), :]
        return far_ref[pl.ds(pl.multiple_of((at + part) * size + rows.start, ROWS), ROWS), :]

    return read


def far_maps(far, link, partner_link):
    size = link.shape[0]

    def kernel(far_ref, link_ref, partner_ref, ll_ref, lr_ref, ul_ref, ur_ref, done_ref, held_ref):
        done_ref[...] = jnp.zeros_like(done_ref)
        position = lax.axis_index("slab")
        upper = position % 2 == 1
        low_at = ((position // 2) * 2).astype(F32)
        count = far_ref[pl.ds(4 * size, EXTRA), :].astype(F32)[:1]
        held_ref[...] = jnp.where(upper, partner_ref[...], link_ref[...])
        put_maps(held_ref, far_block(far_ref, size, 0), low_at < count, ll_ref, lr_ref)
        held_ref[...] = jnp.where(upper, link_ref[...], partner_ref[...])
        put_maps(held_ref, far_block(far_ref, size, 2), low_at + 1 < count, ul_ref, ur_ref)

    maps = jax.ShapeDtypeStruct((2, size, size), BF)
    return call(kernel, [maps] * 4 + [DONE], 8, (), (far, link, partner_link), [pltpu.VMEM(link.shape, BF)])


def far_low(far, left, right, first, second):
    size = left.shape[-1]

    def kernel(far_ref, left_ref, right_ref, a_ref, b_ref, out_ref, middle_ref):
        middle_ref[...] = a_ref[...] + b_ref[...]
        put_sandwich(far_block(far_ref, size, 0), left_ref, right_ref, middle_ref, out_ref)

    return call(kernel, [like(left)], 8, (), (far, left, right, first, second), [pltpu.VMEM(left.shape, BF)])[0]


def far_up(far, left, right, low):
    size = left.shape[-1]

    def kernel(far_ref, left_ref, right_ref, low_ref, mine_ref, *give_refs):
        upper = lax.axis_index("slab") % 2 == 1

        @pl.when(upper)
        def _():
            put_sandwich(far_block(far_ref, size, 2), left_ref, right_ref, low_ref, mine_ref)
            for part in range(2):
                give_refs[part][...] = low_ref[part]

        @pl.when(jnp.logical_not(upper))
        def _():
            put_sandwich(far_block(far_ref, size, 2), left_ref, right_ref, low_ref, give_refs)
            mine_ref[...] = low_ref[...]

    part = jax.ShapeDtypeStruct((size, size), BF)
    return call(kernel, [like(left), part, part], 8, (), (far, left, right, low))


def plan(branch_shift):
    branches = branch_shift.shape[0]

    def kernel(shift_ref, out_ref):
        used = {}
        for d in INNER:
            hit = jnp.int32(0)
            for b in range(branches):
                hit = hit | (shift_ref[b] == d).astype(jnp.int32)
            used[d] = hit
        which = jnp.int32(0)
        for at, held in enumerate(SETS):
            same = jnp.int32(1)
            for d in INNER:
                same = same & (used[d] if d in held else 1 - used[d])
            which = which + same * at
        out_ref[0] = which

    return pl.pallas_call(
        kernel,
        out_shape=jax.ShapeDtypeStruct((1,), jnp.int32),
        in_specs=[SMEM],
        out_specs=SMEM,
        compiler_params=pltpu.CompilerParams(vmem_limit_bytes=GRANT),
    )(branch_shift)


def weights_of(branch_shift, gain):
    branches, size = gain.shape

    def kernel(shift_ref, gain_ref, out_ref, done_ref, gain_t_ref):
        gain_t_ref[...] = gain_ref[...].T
        done_ref[...] = jnp.zeros_like(done_ref)
        energy, energies = lax.axis_index("energy"), lax.axis_size("energy")
        upper = lax.axis_index("slab") % 2 == 1
        first, last = jnp.int32(MAXS), jnp.int32(-MAXS)
        for b in range(branches):
            shift = shift_ref[b]
            inside = (shift > -MAXS) & (shift < MAXS)
            first = jnp.where(inside, jnp.minimum(first, shift), first)
            last = jnp.where(inside, jnp.maximum(last, shift), last)
        side = jnp.where(upper, -MAXS, MAXS)
        none = jnp.int32(10 * MAXS)
        distances = [side, -side, jnp.where(first < MAXS, first, none), jnp.where(last > first, last, none)]
        hits = []
        for distance in distances:
            inside = (energy + distance >= 0) & (energy + distance < energies)
            hits.append([
                jnp.where(inside & (shift_ref[b] == distance), 1.0, 0.0).astype(F32) for b in range(branches)
            ])

        @pl.loop(0, size // 64)
        def _(step):
            rows = pl.ds(pl.multiple_of(step * 64, 64), 64)
            outer = [gain_t_ref[rows, b : b + 1] * gain_ref[b : b + 1, :] for b in range(branches)]
            for k, hit in enumerate(hits):
                out_ref[k, rows, :] = sum(h * o for h, o in zip(hit, outer))

    out = jax.ShapeDtypeStruct((4, size, size), F32)
    return call(kernel, [out, DONE], 0, (branch_shift,), (gain,), [pltpu.VMEM((size, branches), F32)])


def combine(weights, mine, got_real, got_imag, *pieces):
    size = mine.shape[1]

    def kernel(weight_ref, mine_ref, real_ref, imag_ref, *refs):
        @pl.loop(0, size // 64)
        def _(step):
            rows = pl.ds(pl.multiple_of(step * 64, 64), 64)
            held = [weight_ref[k, rows, :] for k in range(2 + len(pieces))]
            for part, got_ref in enumerate((real_ref, imag_ref)):
                blocks = [mine_ref[part, rows, :], got_ref[rows, :]]
                blocks += [ref[part, rows, :] for ref in refs[:-1]]
                total = sum(w * block.astype(F32) for w, block in zip(held, blocks))
                refs[-1][part, rows, :] = total.astype(BF)

    return call(kernel, [like(mine)], 0, (), (weights, mine, got_real, got_imag, *pieces))[0]


def local(inverses, coupling, slab_count, branch_shift, branch_gain):
    block = inverses[:, 0, 0]
    link = coupling[0]
    energies = lax.axis_size("energy")
    slabs = lax.axis_size("slab")
    lows, ups = range(0, slabs, 2), range(1, slabs, 2)

    def moved(value, slab_pairs, distance_of, reach=0):
        route = [
            (((e + distance_of(b)) % energies) * slabs + a, e * slabs + b)
            for e in range(energies)
            for a, b in slab_pairs
            if 0 <= e + reach < energies
        ]
        return lax.ppermute(value, BOTH, route)

    def side(b):
        return MAXS if b % 2 == 0 else -MAXS

    swap = [(i ^ 1, i) for i in range(slabs)]
    same = [(i, i) for i in range(slabs)]

    partner_block = lax.ppermute(block, "slab", swap)
    left, right, both = own_slab(slab_count, block, link, partner_block)
    arrived = lax.ppermute(both, "slab", [(1, 3)])
    later_block, later_link, _ = tie((block, link, both))
    far = message(slab_count, later_block, partner_block)
    partner_link = lax.ppermute(later_link, "slab", swap)

    chip = chip_maps(slab_count, partner_block, partner_link, left, right)
    chip, arrived = tie((chip, arrived))
    green = sandwich(both, *chip, arrived)
    for k in range(3, slabs - 4, 2):
        further = lax.ppermute(green, "slab", [(k, k + 2)])
        if k == 3:
            far = moved(far, same, side)
        green = sandwich(both, *chip, arrived, further)

    to_upper = moved(green, [(b - 2, b) for b in ups if b > 1], side)
    to_lower = moved(green, [(b - 1, b) for b in lows if b > 0], side)

    far, shift, gain, _ = tie((far, branch_shift, branch_gain, green))
    *maps, maps_done = far_maps(far, link, partner_link)
    which = plan(shift)[0]
    weights, weights_done = weights_of(shift, gain)
    to_upper, to_lower, which, _, _ = tie((to_upper, to_lower, which, maps_done, weights_done))

    low = far_low(far, maps[0], maps[1], to_upper, to_lower)
    mine, *give = far_up(far, maps[2], maps[3], low)

    def traded(give):
        return [lax.ppermute(part, "slab", swap) for part in give]

    def alone(weights, mine, *give):
        return combine(weights, mine, *traded(give))

    def relayed(distances):
        def branch(weights, mine, *give):
            pieces = [moved(mine, same, lambda b, d=d: d - side(b), d) for d in distances]
            return combine(weights, mine, *traded(give), *pieces)

        return branch

    branches = [relayed(held) if held else alone for held in SETS]
    sigma = lax.switch(which, branches, weights, mine, *give)
    return sigma[:, None, None]


def solution(mesh):
    return jax.shard_map(
        local,
        mesh=mesh,
        in_specs=(
            P(None, "energy", "slab", None, None),
            P("slab", None, None),
            P("energy"),
            P(),
            P(),
        ),
        out_specs=P(None, "energy", "slab", None, None),
        check_vma=False,
    )
```

```python
import jax
import jax.numpy as jnp
from jax import lax
from jax.experimental import pallas as pl
from jax.experimental.pallas import tpu as pltpu
from jax.sharding import PartitionSpec as P

MAXS = 3
BF = jnp.bfloat16
F32 = jnp.float32
BOTH = ("energy", "slab")
ROWS = 256
EXTRA = 16
GRANT = 24 * 2**20
COST = 1024
tie = lax.optimization_barrier
VMEM = pl.BlockSpec(memory_space=pltpu.VMEM)
SMEM = pl.BlockSpec(memory_space=pltpu.SMEM)
DONE = jax.ShapeDtypeStruct((8, 128), F32)
INNER = list(range(1 - MAXS, MAXS))
SETS = [()] + [(d,) for d in INNER] + [(c, d) for i, c in enumerate(INNER) for d in INNER[i + 1 :]]


def dot(a, b):
    return jnp.dot(a, b, preferred_element_type=F32)


def call(kernel, outs, dots, scalars, arrays, scratch=()):
    return pl.pallas_call(
        kernel,
        out_shape=outs,
        in_specs=[SMEM] * len(scalars) + [VMEM] * len(arrays),
        out_specs=[VMEM] * len(outs),
        scratch_shapes=list(scratch),
        compiler_params=pltpu.CompilerParams(vmem_limit_bytes=GRANT),
        cost_estimate=pl.CostEstimate(
            flops=COST * dots, bytes_accessed=1024, transcendentals=0
        ),
    )(*scalars, *arrays)


def like(array):
    return jax.ShapeDtypeStruct(array.shape, array.dtype)


def steps(size, body):
    @pl.loop(0, size // ROWS)
    def _(step):
        body(pl.ds(pl.multiple_of(step * ROWS, ROWS), ROWS))


def put_maps(link_ref, block, on, left_ref, right_ref):
    def body(rows):
        for part in range(2):
            left = dot(block(part, rows), link_ref[...])
            left_ref[part, rows, :] = jnp.where(on, left, 0.0).astype(BF)
            right = lax.dot_general(
                link_ref[:, rows],
                block(part, slice(None)),
                (((0,), (0,)), ((), ())),
                preferred_element_type=F32,
            )
            right_ref[part, rows, :] = jnp.where(on, right, 0.0).astype(BF)

    steps(link_ref.shape[0], body)


def complex_rows(a_ref, rows, b_ref):
    ar, ai = a_ref[0, rows, :], a_ref[1, rows, :]
    return dot(ar, b_ref[0]) - dot(ai, b_ref[1]), dot(ar, b_ref[1]) + dot(ai, b_ref[0])


def put_sandwich(base, left_ref, right_ref, middle_ref, out_ref):
    def body(rows):
        hr, hi = complex_rows(left_ref, rows, middle_ref)
        hr, hi = hr.astype(BF), hi.astype(BF)
        rr, ri = right_ref[0], right_ref[1]
        parts[0][rows, :] = (base(0, rows).astype(F32) + dot(hr, rr) - dot(hi, ri)).astype(BF)
        parts[1][rows, :] = (base(1, rows).astype(F32) + dot(hr, ri) + dot(hi, rr)).astype(BF)

    parts = out_ref if isinstance(out_ref, tuple) else (out_ref.at[0], out_ref.at[1])
    steps(parts[0].shape[0], body)


def reader(ref, at=0):
    return lambda part, rows: ref[at + part, rows, :]


def staged(block, link):
    def kernel(block_ref, link_ref, block_out, link_out):
        block_out[...] = block_ref[...]
        link_out[...] = link_ref[...]

    return call(kernel, [like(block), like(link)], 0, (), (block, link))


def own_slab(slab_count, block, link, partner_block):
    def kernel(count_ref, block_ref, link_ref, partner_ref, left_ref, right_ref, both_ref):
        on = lax.axis_index("slab") < count_ref[0]
        put_maps(link_ref, reader(block_ref), on, left_ref, right_ref)
        put_sandwich(reader(block_ref), left_ref, right_ref, partner_ref, both_ref)

    return call(kernel, [like(block)] * 3, 12, (slab_count,), (block, link, partner_block))


def chip_maps(slab_count, partner_block, partner_link, left, right):
    def kernel(count_ref, block_ref, link_ref, l_ref, r_ref, left_ref, right_ref, ol_ref, or_ref):
        on = (lax.axis_index("slab") ^ 1) < count_ref[0]
        put_maps(link_ref, reader(block_ref), on, ol_ref, or_ref)

        def body(rows):
            for a_ref, b_ref, o_ref in ((l_ref, ol_ref, left_ref), (or_ref, r_ref, right_ref)):
                real, imag = complex_rows(a_ref, rows, b_ref)
                o_ref[0, rows, :] = real.astype(BF)
                o_ref[1, rows, :] = imag.astype(BF)

        steps(left.shape[1], body)

    scratch = [pltpu.VMEM(left.shape, BF)] * 2
    return call(kernel, [like(left)] * 2, 12, (slab_count,), (partner_block, partner_link, left, right), scratch)


def sandwich(base, left, right, *middles):
    def kernel(base_ref, left_ref, right_ref, *refs):
        middle_ref, out_ref = refs[0], refs[len(middles)]
        if len(middles) > 1:
            middle_ref = refs[-1]
            middle_ref[...] = refs[0][...] + refs[1][...]
        put_sandwich(reader(base_ref), left_ref, right_ref, middle_ref, out_ref)

    scratch = [pltpu.VMEM(base.shape, BF)] * (len(middles) > 1)
    return call(kernel, [like(base)], 8, (), (base, left, right, *middles), scratch)[0]


def message(slab_count, block, partner_block):
    size = block.shape[1]

    def kernel(count_ref, block_ref, partner_ref, out_ref):
        upper = lax.axis_index("slab") % 2 == 1
        low = jnp.where(upper, partner_ref[...], block_ref[...])
        high = jnp.where(upper, block_ref[...], partner_ref[...])
        for part in range(2):
            out_ref[pl.ds(part * size, size), :] = low[part]
            out_ref[pl.ds((2 + part) * size, size), :] = high[part]
        count = jnp.full((EXTRA, size), count_ref[0], jnp.int32).astype(F32)
        out_ref[pl.ds(4 * size, EXTRA), :] = count.astype(BF)

    out = jax.ShapeDtypeStruct((4 * size + EXTRA, size), BF)
    return call(kernel, [out], 0, (slab_count,), (block, partner_block))[0]


def far_block(far_ref, size, at):
    def read(part, rows):
        if isinstance(rows, slice):
            return far_ref[pl.ds((at + part) * size, size), :]
        return far_ref[pl.ds(pl.multiple_of((at + part) * size + rows.start, ROWS), ROWS), :]

    return read


def far_maps(far, link, partner_link):
    size = link.shape[0]

    def kernel(far_ref, link_ref, partner_ref, ll_ref, lr_ref, ul_ref, ur_ref, done_ref, held_ref):
        done_ref[...] = jnp.zeros_like(done_ref)
        position = lax.axis_index("slab")
        upper = position % 2 == 1
        low_at = ((position // 2) * 2).astype(F32)
        count = far_ref[pl.ds(4 * size, EXTRA), :].astype(F32)[:1]
        held_ref[...] = jnp.where(upper, partner_ref[...], link_ref[...])
        put_maps(held_ref, far_block(far_ref, size, 0), low_at < count, ll_ref, lr_ref)
        held_ref[...] = jnp.where(upper, link_ref[...], partner_ref[...])
        put_maps(held_ref, far_block(far_ref, size, 2), low_at + 1 < count, ul_ref, ur_ref)

    maps = jax.ShapeDtypeStruct((2, size, size), BF)
    return call(kernel, [maps] * 4 + [DONE], 8, (), (far, link, partner_link), [pltpu.VMEM(link.shape, BF)])


def far_low(far, left, right, first, second):
    size = left.shape[-1]

    def kernel(far_ref, left_ref, right_ref, a_ref, b_ref, out_ref, middle_ref):
        middle_ref[...] = a_ref[...] + b_ref[...]
        put_sandwich(far_block(far_ref, size, 0), left_ref, right_ref, middle_ref, out_ref)

    return call(kernel, [like(left)], 8, (), (far, left, right, first, second), [pltpu.VMEM(left.shape, BF)])[0]


def far_up(far, left, right, low):
    size = left.shape[-1]

    def kernel(far_ref, left_ref, right_ref, low_ref, mine_ref, *give_refs):
        upper = lax.axis_index("slab") % 2 == 1

        @pl.when(upper)
        def _():
            put_sandwich(far_block(far_ref, size, 2), left_ref, right_ref, low_ref, mine_ref)
            for part in range(2):
                give_refs[part][...] = low_ref[part]

        @pl.when(jnp.logical_not(upper))
        def _():
            put_sandwich(far_block(far_ref, size, 2), left_ref, right_ref, low_ref, give_refs)
            mine_ref[...] = low_ref[...]

    part = jax.ShapeDtypeStruct((size, size), BF)
    return call(kernel, [like(left), part, part], 8, (), (far, left, right, low))


def plan(branch_shift):
    branches = branch_shift.shape[0]

    def kernel(shift_ref, out_ref):
        used = {}
        for d in INNER:
            hit = jnp.int32(0)
            for b in range(branches):
                hit = hit | (shift_ref[b] == d).astype(jnp.int32)
            used[d] = hit
        which = jnp.int32(0)
        for at, held in enumerate(SETS):
            same = jnp.int32(1)
            for d in INNER:
                same = same & (used[d] if d in held else 1 - used[d])
            which = which + same * at
        out_ref[0] = which

    return pl.pallas_call(
        kernel,
        out_shape=jax.ShapeDtypeStruct((1,), jnp.int32),
        in_specs=[SMEM],
        out_specs=SMEM,
        compiler_params=pltpu.CompilerParams(vmem_limit_bytes=GRANT),
    )(branch_shift)


def weights_of(branch_shift, gain):
    branches, size = gain.shape

    def kernel(shift_ref, gain_ref, out_ref, done_ref, gain_t_ref):
        gain_t_ref[...] = gain_ref[...].T
        done_ref[...] = jnp.zeros_like(done_ref)
        energy, energies = lax.axis_index("energy"), lax.axis_size("energy")
        upper = lax.axis_index("slab") % 2 == 1
        first, last = jnp.int32(MAXS), jnp.int32(-MAXS)
        for b in range(branches):
            shift = shift_ref[b]
            inside = (shift > -MAXS) & (shift < MAXS)
            first = jnp.where(inside, jnp.minimum(first, shift), first)
            last = jnp.where(inside, jnp.maximum(last, shift), last)
        side = jnp.where(upper, -MAXS, MAXS)
        none = jnp.int32(10 * MAXS)
        distances = [side, -side, jnp.where(first < MAXS, first, none), jnp.where(last > first, last, none)]
        hits = []
        for distance in distances:
            inside = (energy + distance >= 0) & (energy + distance < energies)
            hits.append([
                jnp.where(inside & (shift_ref[b] == distance), 1.0, 0.0).astype(F32) for b in range(branches)
            ])

        @pl.loop(0, size // 64)
        def _(step):
            rows = pl.ds(pl.multiple_of(step * 64, 64), 64)
            outer = [gain_t_ref[rows, b : b + 1] * gain_ref[b : b + 1, :] for b in range(branches)]
            for k, hit in enumerate(hits):
                out_ref[k, rows, :] = sum(h * o for h, o in zip(hit, outer))

    out = jax.ShapeDtypeStruct((4, size, size), F32)
    return call(kernel, [out, DONE], 0, (branch_shift,), (gain,), [pltpu.VMEM((size, branches), F32)])


def combine(weights, mine, got_real, got_imag, *pieces):
    size = mine.shape[1]

    def kernel(weight_ref, mine_ref, real_ref, imag_ref, *refs):
        @pl.loop(0, size // 64)
        def _(step):
            rows = pl.ds(pl.multiple_of(step * 64, 64), 64)
            held = [weight_ref[k, rows, :] for k in range(2 + len(pieces))]
            for part, got_ref in enumerate((real_ref, imag_ref)):
                blocks = [mine_ref[part, rows, :], got_ref[rows, :]]
                blocks += [ref[part, rows, :] for ref in refs[:-1]]
                total = sum(w * block.astype(F32) for w, block in zip(held, blocks))
                refs[-1][part, rows, :] = total.astype(BF)

    return call(kernel, [like(mine)], 0, (), (weights, mine, got_real, got_imag, *pieces))[0]


def local(inverses, coupling, slab_count, branch_shift, branch_gain):
    block = inverses[:, 0, 0]
    link = coupling[0]
    energies = lax.axis_size("energy")
    slabs = lax.axis_size("slab")
    lows, ups = range(0, slabs, 2), range(1, slabs, 2)

    def moved(value, slab_pairs, distance_of, reach=0):
        route = [
            (((e + distance_of(b)) % energies) * slabs + a, e * slabs + b)
            for e in range(energies)
            for a, b in slab_pairs
            if 0 <= e + reach < energies
        ]
        return lax.ppermute(value, BOTH, route)

    def side(b):
        return MAXS if b % 2 == 0 else -MAXS

    swap = [(i ^ 1, i) for i in range(slabs)]
    same = [(i, i) for i in range(slabs)]

    partner_block = lax.ppermute(block, "slab", swap)
    block, link = staged(block, link)
    left, right, both = own_slab(slab_count, block, link, partner_block)
    arrived = lax.ppermute(both, "slab", [(1, 3)])
    later_block, later_link, _ = tie((block, link, both))
    far = message(slab_count, later_block, partner_block)
    partner_link = lax.ppermute(later_link, "slab", swap)

    chip = chip_maps(slab_count, partner_block, partner_link, left, right)
    chip, arrived = tie((chip, arrived))
    green = sandwich(both, *chip, arrived)
    for k in range(3, slabs - 4, 2):
        further = lax.ppermute(green, "slab", [(k, k + 2)])
        if k == 3:
            far = moved(far, same, side)
        green = sandwich(both, *chip, arrived, further)

    to_upper = moved(green, [(b - 2, b) for b in ups if b > 1], side)
    to_lower = moved(green, [(b - 1, b) for b in lows if b > 0], side)

    far, shift, gain, _ = tie((far, branch_shift, branch_gain, green))
    *maps, maps_done = far_maps(far, link, partner_link)
    which = plan(shift)[0]
    weights, weights_done = weights_of(shift, gain)
    to_upper, to_lower, which, _, _ = tie((to_upper, to_lower, which, maps_done, weights_done))

    low = far_low(far, maps[0], maps[1], to_upper, to_lower)
    mine, *give = far_up(far, maps[2], maps[3], low)

    def traded(give):
        return [lax.ppermute(part, "slab", swap) for part in give]

    def alone(weights, mine, *give):
        return combine(weights, mine, *traded(give))

    def relayed(distances):
        def branch(weights, mine, *give):
            pieces = [moved(mine, same, lambda b, d=d: d - side(b), d) for d in distances]
            return combine(weights, mine, *traded(give), *pieces)

        return branch

    branches = [relayed(held) if held else alone for held in SETS]
    sigma = lax.switch(which, branches, weights, mine, *give)
    return sigma[:, None, None]


def solution(mesh):
    return jax.shard_map(
        local,
        mesh=mesh,
        in_specs=(
            P(None, "energy", "slab", None, None),
            P("slab", None, None),
            P("energy"),
            P(),
            P(),
        ),
        out_specs=P(None, "energy", "slab", None, None),
        check_vma=False,
    )
```

```python
import jax
import jax.numpy as jnp
from jax import lax
from jax.experimental import pallas as pl
from jax.experimental.pallas import tpu as pltpu
from jax.sharding import PartitionSpec as P

MAXS = 3
BF = jnp.bfloat16
F32 = jnp.float32
BOTH = ("energy", "slab")
ROWS = 256
EXTRA = 16
GRANT = 24 * 2**20
COST = 1024
tie = lax.optimization_barrier
VMEM = pl.BlockSpec(memory_space=pltpu.VMEM)
SMEM = pl.BlockSpec(memory_space=pltpu.SMEM)
DONE = jax.ShapeDtypeStruct((8, 128), F32)
INNER = list(range(1 - MAXS, MAXS))
SETS = [()] + [(d,) for d in INNER] + [(c, d) for i, c in enumerate(INNER) for d in INNER[i + 1 :]]


def dot(a, b):
    return jnp.dot(a, b, preferred_element_type=F32)


def call(kernel, outs, dots, scalars, arrays, scratch=()):
    return pl.pallas_call(
        kernel,
        out_shape=outs,
        in_specs=[SMEM] * len(scalars) + [VMEM] * len(arrays),
        out_specs=[VMEM] * len(outs),
        scratch_shapes=list(scratch),
        compiler_params=pltpu.CompilerParams(vmem_limit_bytes=GRANT),
        cost_estimate=pl.CostEstimate(
            flops=COST * dots, bytes_accessed=1024, transcendentals=0
        ),
    )(*scalars, *arrays)


def like(array):
    return jax.ShapeDtypeStruct(array.shape, array.dtype)


def steps(size, body):
    @pl.loop(0, size // ROWS)
    def _(step):
        body(pl.ds(pl.multiple_of(step * ROWS, ROWS), ROWS))


def put_maps(link_ref, block, on, left_ref, right_ref):
    def body(rows):
        for part in range(2):
            left = dot(block(part, rows), link_ref[...])
            left_ref[part, rows, :] = jnp.where(on, left, 0.0).astype(BF)
            right = lax.dot_general(
                link_ref[:, rows],
                block(part, slice(None)),
                (((0,), (0,)), ((), ())),
                preferred_element_type=F32,
            )
            right_ref[part, rows, :] = jnp.where(on, right, 0.0).astype(BF)

    steps(link_ref.shape[0], body)


def complex_rows(a_ref, rows, b_ref):
    ar, ai = a_ref[0, rows, :], a_ref[1, rows, :]
    return dot(ar, b_ref[0]) - dot(ai, b_ref[1]), dot(ar, b_ref[1]) + dot(ai, b_ref[0])


def put_sandwich(base, left_ref, right_ref, middle_ref, out_ref):
    def body(rows):
        hr, hi = complex_rows(left_ref, rows, middle_ref)
        hr, hi = hr.astype(BF), hi.astype(BF)
        rr, ri = right_ref[0], right_ref[1]
        parts[0][rows, :] = (base(0, rows).astype(F32) + dot(hr, rr) - dot(hi, ri)).astype(BF)
        parts[1][rows, :] = (base(1, rows).astype(F32) + dot(hr, ri) + dot(hi, rr)).astype(BF)

    parts = out_ref if isinstance(out_ref, tuple) else (out_ref.at[0], out_ref.at[1])
    steps(parts[0].shape[0], body)


def reader(ref, at=0):
    return lambda part, rows: ref[at + part, rows, :]


def staged(block, link):
    def kernel(block_ref, link_ref, block_out, link_out):
        block_out[...] = block_ref[...]
        link_out[...] = link_ref[...]

    return call(kernel, [like(block), like(link)], 0, (), (block, link))


def own_slab(slab_count, block, link, partner_block):
    def kernel(count_ref, block_ref, link_ref, partner_ref, left_ref, right_ref, both_ref):
        on = lax.axis_index("slab") < count_ref[0]
        put_maps(link_ref, reader(block_ref), on, left_ref, right_ref)
        put_sandwich(reader(block_ref), left_ref, right_ref, partner_ref, both_ref)

    return call(kernel, [like(block)] * 3, 12, (slab_count,), (block, link, partner_block))


def chip_maps(slab_count, partner_block, partner_link, left, right):
    def kernel(count_ref, block_ref, link_ref, l_ref, r_ref, left_ref, right_ref, ol_ref, or_ref):
        on = (lax.axis_index("slab") ^ 1) < count_ref[0]
        put_maps(link_ref, reader(block_ref), on, ol_ref, or_ref)

        def body(rows):
            for a_ref, b_ref, o_ref in ((l_ref, ol_ref, left_ref), (or_ref, r_ref, right_ref)):
                real, imag = complex_rows(a_ref, rows, b_ref)
                o_ref[0, rows, :] = real.astype(BF)
                o_ref[1, rows, :] = imag.astype(BF)

        steps(left.shape[1], body)

    scratch = [pltpu.VMEM(left.shape, BF)] * 2
    return call(kernel, [like(left)] * 2, 12, (slab_count,), (partner_block, partner_link, left, right), scratch)


def sandwich(base, left, right, *middles):
    def kernel(base_ref, left_ref, right_ref, *refs):
        middle_ref, out_ref = refs[0], refs[len(middles)]
        if len(middles) > 1:
            middle_ref = refs[-1]
            middle_ref[...] = refs[0][...] + refs[1][...]
        put_sandwich(reader(base_ref), left_ref, right_ref, middle_ref, out_ref)

    scratch = [pltpu.VMEM(base.shape, BF)] * (len(middles) > 1)
    return call(kernel, [like(base)], 8, (), (base, left, right, *middles), scratch)[0]


def message(slab_count, block, partner_block):
    size = block.shape[1]

    def kernel(count_ref, block_ref, partner_ref, out_ref):
        upper = lax.axis_index("slab") % 2 == 1
        low = jnp.where(upper, partner_ref[...], block_ref[...])
        high = jnp.where(upper, block_ref[...], partner_ref[...])
        for part in range(2):
            out_ref[pl.ds(part * size, size), :] = low[part]
            out_ref[pl.ds((2 + part) * size, size), :] = high[part]
        count = jnp.full((EXTRA, size), count_ref[0], jnp.int32).astype(F32)
        out_ref[pl.ds(4 * size, EXTRA), :] = count.astype(BF)

    out = jax.ShapeDtypeStruct((4 * size + EXTRA, size), BF)
    return call(kernel, [out], 0, (slab_count,), (block, partner_block))[0]


def far_block(far_ref, size, at):
    def read(part, rows):
        if isinstance(rows, slice):
            return far_ref[pl.ds((at + part) * size, size), :]
        return far_ref[pl.ds(pl.multiple_of((at + part) * size + rows.start, ROWS), ROWS), :]

    return read


def far_maps(far, link, partner_link):
    size = link.shape[0]

    def kernel(far_ref, link_ref, partner_ref, ll_ref, lr_ref, ul_ref, ur_ref, done_ref, held_ref):
        done_ref[...] = jnp.zeros_like(done_ref)
        position = lax.axis_index("slab")
        upper = position % 2 == 1
        low_at = ((position // 2) * 2).astype(F32)
        count = far_ref[pl.ds(4 * size, EXTRA), :].astype(F32)[:1]
        held_ref[...] = jnp.where(upper, partner_ref[...], link_ref[...])
        put_maps(held_ref, far_block(far_ref, size, 0), low_at < count, ll_ref, lr_ref)
        held_ref[...] = jnp.where(upper, link_ref[...], partner_ref[...])
        put_maps(held_ref, far_block(far_ref, size, 2), low_at + 1 < count, ul_ref, ur_ref)

    maps = jax.ShapeDtypeStruct((2, size, size), BF)
    return call(kernel, [maps] * 4 + [DONE], 8, (), (far, link, partner_link), [pltpu.VMEM(link.shape, BF)])


def far_low(far, left, right, first, second):
    size = left.shape[-1]

    def kernel(far_ref, left_ref, right_ref, a_ref, b_ref, out_ref, middle_ref):
        middle_ref[...] = a_ref[...] + b_ref[...]
        put_sandwich(far_block(far_ref, size, 0), left_ref, right_ref, middle_ref, out_ref)

    return call(kernel, [like(left)], 8, (), (far, left, right, first, second), [pltpu.VMEM(left.shape, BF)])[0]


def far_up(far, left, right, low):
    size = left.shape[-1]

    def kernel(far_ref, left_ref, right_ref, low_ref, mine_ref, *give_refs):
        upper = lax.axis_index("slab") % 2 == 1

        @pl.when(upper)
        def _():
            put_sandwich(far_block(far_ref, size, 2), left_ref, right_ref, low_ref, mine_ref)
            for part in range(2):
                give_refs[part][...] = low_ref[part]

        @pl.when(jnp.logical_not(upper))
        def _():
            put_sandwich(far_block(far_ref, size, 2), left_ref, right_ref, low_ref, give_refs)
            mine_ref[...] = low_ref[...]

    part = jax.ShapeDtypeStruct((size, size), BF)
    return call(kernel, [like(left), part, part], 8, (), (far, left, right, low))


def plan(branch_shift):
    branches = branch_shift.shape[0]

    def kernel(shift_ref, out_ref):
        used = {}
        for d in INNER:
            hit = jnp.int32(0)
            for b in range(branches):
                hit = hit | (shift_ref[b] == d).astype(jnp.int32)
            used[d] = hit
        which = jnp.int32(0)
        for at, held in enumerate(SETS):
            same = jnp.int32(1)
            for d in INNER:
                same = same & (used[d] if d in held else 1 - used[d])
            which = which + same * at
        out_ref[0] = which

    return pl.pallas_call(
        kernel,
        out_shape=jax.ShapeDtypeStruct((1,), jnp.int32),
        in_specs=[SMEM],
        out_specs=SMEM,
        compiler_params=pltpu.CompilerParams(vmem_limit_bytes=GRANT),
    )(branch_shift)


def weights_of(branch_shift, gain):
    branches, size = gain.shape

    def kernel(shift_ref, gain_ref, *refs):
        *out_refs, done_ref, gain_t_ref = refs
        gain_t_ref[...] = gain_ref[...].T
        done_ref[...] = jnp.zeros_like(done_ref)
        energy, energies = lax.axis_index("energy"), lax.axis_size("energy")
        upper = lax.axis_index("slab") % 2 == 1
        first, last = jnp.int32(MAXS), jnp.int32(-MAXS)
        for b in range(branches):
            shift = shift_ref[b]
            inside = (shift > -MAXS) & (shift < MAXS)
            first = jnp.where(inside, jnp.minimum(first, shift), first)
            last = jnp.where(inside, jnp.maximum(last, shift), last)
        side = jnp.where(upper, -MAXS, MAXS)
        none = jnp.int32(10 * MAXS)
        distances = [side, -side, jnp.where(first < MAXS, first, none), jnp.where(last > first, last, none)]
        hits = []
        for distance in distances:
            inside = (energy + distance >= 0) & (energy + distance < energies)
            hits.append([
                jnp.where(inside & (shift_ref[b] == distance), 1.0, 0.0).astype(F32) for b in range(branches)
            ])

        @pl.loop(0, size // 64)
        def _(step):
            rows = pl.ds(pl.multiple_of(step * 64, 64), 64)
            outer = [gain_t_ref[rows, b : b + 1] * gain_ref[b : b + 1, :] for b in range(branches)]
            for out_ref, hit in zip(out_refs, hits):
                out_ref[rows, :] = sum(h * o for h, o in zip(hit, outer))

    out = jax.ShapeDtypeStruct((size, size), F32)
    return call(kernel, [out] * 4 + [DONE], 0, (branch_shift,), (gain,), [pltpu.VMEM((size, branches), F32)])


def combine(weights, mine, got_real, got_imag, *pieces):
    size = mine.shape[1]

    def kernel(*refs):
        weight_refs, (mine_ref, real_ref, imag_ref, *refs) = refs[: len(weights)], refs[len(weights) :]
        @pl.loop(0, size // 64)
        def _(step):
            rows = pl.ds(pl.multiple_of(step * 64, 64), 64)
            held = [weight_ref[rows, :] for weight_ref in weight_refs]
            for part, got_ref in enumerate((real_ref, imag_ref)):
                blocks = [mine_ref[part, rows, :], got_ref[rows, :]]
                blocks += [ref[part, rows, :] for ref in refs[:-1]]
                total = sum(w * block.astype(F32) for w, block in zip(held, blocks))
                refs[-1][part, rows, :] = total.astype(BF)

    return call(kernel, [like(mine)], 0, (), (*weights, mine, got_real, got_imag, *pieces))[0]


def local(inverses, coupling, slab_count, branch_shift, branch_gain):
    block = inverses[:, 0, 0]
    link = coupling[0]
    energies = lax.axis_size("energy")
    slabs = lax.axis_size("slab")
    lows, ups = range(0, slabs, 2), range(1, slabs, 2)

    def moved(value, slab_pairs, distance_of, reach=0):
        route = [
            (((e + distance_of(b)) % energies) * slabs + a, e * slabs + b)
            for e in range(energies)
            for a, b in slab_pairs
            if 0 <= e + reach < energies
        ]
        return lax.ppermute(value, BOTH, route)

    def side(b):
        return MAXS if b % 2 == 0 else -MAXS

    swap = [(i ^ 1, i) for i in range(slabs)]
    same = [(i, i) for i in range(slabs)]

    partner_block = lax.ppermute(block, "slab", swap)
    block, link = staged(block, link)
    left, right, both = own_slab(slab_count, block, link, partner_block)
    arrived = lax.ppermute(both, "slab", [(1, 3)])
    later_block, later_link, _ = tie((block, link, both))
    far = message(slab_count, later_block, partner_block)
    partner_link = lax.ppermute(later_link, "slab", swap)

    chip = chip_maps(slab_count, partner_block, partner_link, left, right)
    chip, arrived = tie((chip, arrived))
    green = sandwich(both, *chip, arrived)
    for k in range(3, slabs - 4, 2):
        further = lax.ppermute(green, "slab", [(k, k + 2)])
        if k == 3:
            far = moved(far, same, side)
        green = sandwich(both, *chip, arrived, further)

    to_upper = moved(green, [(b - 2, b) for b in ups if b > 1], side)
    to_lower = moved(green, [(b - 1, b) for b in lows if b > 0], side)

    far, shift, gain, _ = tie((far, branch_shift, branch_gain, green))
    *maps, maps_done = far_maps(far, link, partner_link)
    which = plan(shift)[0]
    *weights, weights_done = weights_of(shift, gain)
    to_upper, to_lower, which, _, _ = tie((to_upper, to_lower, which, maps_done, weights_done))

    low = far_low(far, maps[0], maps[1], to_upper, to_lower)
    mine, *give = far_up(far, maps[2], maps[3], low)

    def traded(give):
        return [lax.ppermute(part, "slab", swap) for part in give]

    def alone(weights, mine, *give):
        return combine(weights[:2], mine, *traded(give))

    def relayed(distances):
        def branch(weights, mine, *give):
            pieces = [moved(mine, same, lambda b, d=d: d - side(b), d) for d in distances]
            return combine(weights[: 2 + len(pieces)], mine, *traded(give), *pieces)

        return branch

    branches = [relayed(held) if held else alone for held in SETS]
    sigma = lax.switch(which, branches, weights, mine, *give)
    return sigma[:, None, None]


def solution(mesh):
    return jax.shard_map(
        local,
        mesh=mesh,
        in_specs=(
            P(None, "energy", "slab", None, None),
            P("slab", None, None),
            P("energy"),
            P(),
            P(),
        ),
        out_specs=P(None, "energy", "slab", None, None),
        check_vma=False,
    )
```

```python
import jax
import jax.numpy as jnp
from jax import lax
from jax.experimental import pallas as pl
from jax.experimental.pallas import tpu as pltpu
from jax.sharding import PartitionSpec as P

MAXS = 3
BF = jnp.bfloat16
F32 = jnp.float32
BOTH = ("energy", "slab")
ROWS = 512
EXTRA = 16
GRANT = 24 * 2**20
COST = 1024
tie = lax.optimization_barrier
VMEM = pl.BlockSpec(memory_space=pltpu.VMEM)
SMEM = pl.BlockSpec(memory_space=pltpu.SMEM)
DONE = jax.ShapeDtypeStruct((8, 128), F32)
INNER = list(range(1 - MAXS, MAXS))
SETS = [()] + [(d,) for d in INNER] + [(c, d) for i, c in enumerate(INNER) for d in INNER[i + 1 :]]


def dot(a, b):
    return jnp.dot(a, b, preferred_element_type=F32)


def call(kernel, outs, dots, scalars, arrays, scratch=()):
    return pl.pallas_call(
        kernel,
        out_shape=outs,
        in_specs=[SMEM] * len(scalars) + [VMEM] * len(arrays),
        out_specs=[VMEM] * len(outs),
        scratch_shapes=list(scratch),
        compiler_params=pltpu.CompilerParams(vmem_limit_bytes=GRANT),
        cost_estimate=pl.CostEstimate(
            flops=COST * dots, bytes_accessed=1024, transcendentals=0
        ),
    )(*scalars, *arrays)


def like(array):
    return jax.ShapeDtypeStruct(array.shape, array.dtype)


def steps(size, body):
    @pl.loop(0, size // ROWS)
    def _(step):
        body(pl.ds(pl.multiple_of(step * ROWS, ROWS), ROWS))


def put_maps(link_ref, block, on, left_ref, right_ref):
    def body(rows):
        for part in range(2):
            left = dot(block(part, rows), link_ref[...])
            left_ref[part, rows, :] = jnp.where(on, left, 0.0).astype(BF)
            right = lax.dot_general(
                link_ref[:, rows],
                block(part, slice(None)),
                (((0,), (0,)), ((), ())),
                preferred_element_type=F32,
            )
            right_ref[part, rows, :] = jnp.where(on, right, 0.0).astype(BF)

    steps(link_ref.shape[0], body)


def complex_rows(a_ref, rows, b_ref):
    ar, ai = a_ref[0, rows, :], a_ref[1, rows, :]
    return dot(ar, b_ref[0]) - dot(ai, b_ref[1]), dot(ar, b_ref[1]) + dot(ai, b_ref[0])


def put_sandwich(base, left_ref, right_ref, middle_ref, out_ref):
    def body(rows):
        hr, hi = complex_rows(left_ref, rows, middle_ref)
        hr, hi = hr.astype(BF), hi.astype(BF)
        rr, ri = right_ref[0], right_ref[1]
        parts[0][rows, :] = (base(0, rows).astype(F32) + dot(hr, rr) - dot(hi, ri)).astype(BF)
        parts[1][rows, :] = (base(1, rows).astype(F32) + dot(hr, ri) + dot(hi, rr)).astype(BF)

    parts = out_ref if isinstance(out_ref, tuple) else (out_ref.at[0], out_ref.at[1])
    steps(parts[0].shape[0], body)


def reader(ref, at=0):
    return lambda part, rows: ref[at + part, rows, :]


def staged(block, link):
    def kernel(block_ref, link_ref, block_out, link_out):
        block_out[...] = block_ref[...]
        link_out[...] = link_ref[...]

    return call(kernel, [like(block), like(link)], 0, (), (block, link))


def own_slab(slab_count, block, link, partner_block):
    def kernel(count_ref, block_ref, link_ref, partner_ref, left_ref, right_ref, both_ref):
        on = lax.axis_index("slab") < count_ref[0]
        put_maps(link_ref, reader(block_ref), on, left_ref, right_ref)
        put_sandwich(reader(block_ref), left_ref, right_ref, partner_ref, both_ref)

    return call(kernel, [like(block)] * 3, 12, (slab_count,), (block, link, partner_block))


def chip_maps(slab_count, partner_block, partner_link, left, right):
    def kernel(count_ref, block_ref, link_ref, l_ref, r_ref, left_ref, right_ref, ol_ref, or_ref):
        on = (lax.axis_index("slab") ^ 1) < count_ref[0]
        put_maps(link_ref, reader(block_ref), on, ol_ref, or_ref)

        def body(rows):
            for a_ref, b_ref, o_ref in ((l_ref, ol_ref, left_ref), (or_ref, r_ref, right_ref)):
                real, imag = complex_rows(a_ref, rows, b_ref)
                o_ref[0, rows, :] = real.astype(BF)
                o_ref[1, rows, :] = imag.astype(BF)

        steps(left.shape[1], body)

    scratch = [pltpu.VMEM(left.shape, BF)] * 2
    return call(kernel, [like(left)] * 2, 12, (slab_count,), (partner_block, partner_link, left, right), scratch)


def sandwich(base, left, right, *middles):
    def kernel(base_ref, left_ref, right_ref, *refs):
        middle_ref, out_ref = refs[0], refs[len(middles)]
        if len(middles) > 1:
            middle_ref = refs[-1]
            middle_ref[...] = refs[0][...] + refs[1][...]
        put_sandwich(reader(base_ref), left_ref, right_ref, middle_ref, out_ref)

    scratch = [pltpu.VMEM(base.shape, BF)] * (len(middles) > 1)
    return call(kernel, [like(base)], 8, (), (base, left, right, *middles), scratch)[0]


def message(slab_count, block, partner_block):
    size = block.shape[1]

    def kernel(count_ref, block_ref, partner_ref, out_ref):
        upper = lax.axis_index("slab") % 2 == 1
        low = jnp.where(upper, partner_ref[...], block_ref[...])
        high = jnp.where(upper, block_ref[...], partner_ref[...])
        for part in range(2):
            out_ref[pl.ds(part * size, size), :] = low[part]
            out_ref[pl.ds((2 + part) * size, size), :] = high[part]
        count = jnp.full((EXTRA, size), count_ref[0], jnp.int32).astype(F32)
        out_ref[pl.ds(4 * size, EXTRA), :] = count.astype(BF)

    out = jax.ShapeDtypeStruct((4 * size + EXTRA, size), BF)
    return call(kernel, [out], 0, (slab_count,), (block, partner_block))[0]


def far_block(far_ref, size, at):
    def read(part, rows):
        if isinstance(rows, slice):
            return far_ref[pl.ds((at + part) * size, size), :]
        return far_ref[pl.ds(pl.multiple_of((at + part) * size + rows.start, ROWS), ROWS), :]

    return read


def far_maps(far, link, partner_link):
    size = link.shape[0]

    def kernel(far_ref, link_ref, partner_ref, ll_ref, lr_ref, ul_ref, ur_ref, done_ref, held_ref):
        done_ref[...] = jnp.zeros_like(done_ref)
        position = lax.axis_index("slab")
        upper = position % 2 == 1
        low_at = ((position // 2) * 2).astype(F32)
        count = far_ref[pl.ds(4 * size, EXTRA), :].astype(F32)[:1]
        held_ref[...] = jnp.where(upper, partner_ref[...], link_ref[...])
        put_maps(held_ref, far_block(far_ref, size, 0), low_at < count, ll_ref, lr_ref)
        held_ref[...] = jnp.where(upper, link_ref[...], partner_ref[...])
        put_maps(held_ref, far_block(far_ref, size, 2), low_at + 1 < count, ul_ref, ur_ref)

    maps = jax.ShapeDtypeStruct((2, size, size), BF)
    return call(kernel, [maps] * 4 + [DONE], 8, (), (far, link, partner_link), [pltpu.VMEM(link.shape, BF)])


def far_low(far, left, right, first, second):
    size = left.shape[-1]

    def kernel(far_ref, left_ref, right_ref, a_ref, b_ref, out_ref, middle_ref):
        middle_ref[...] = a_ref[...] + b_ref[...]
        put_sandwich(far_block(far_ref, size, 0), left_ref, right_ref, middle_ref, out_ref)

    return call(kernel, [like(left)], 8, (), (far, left, right, first, second), [pltpu.VMEM(left.shape, BF)])[0]


def far_up(far, left, right, low):
    size = left.shape[-1]

    def kernel(far_ref, left_ref, right_ref, low_ref, mine_ref, *give_refs):
        upper = lax.axis_index("slab") % 2 == 1

        @pl.when(upper)
        def _():
            put_sandwich(far_block(far_ref, size, 2), left_ref, right_ref, low_ref, mine_ref)
            for part in range(2):
                give_refs[part][...] = low_ref[part]

        @pl.when(jnp.logical_not(upper))
        def _():
            put_sandwich(far_block(far_ref, size, 2), left_ref, right_ref, low_ref, give_refs)
            mine_ref[...] = low_ref[...]

    part = jax.ShapeDtypeStruct((size, size), BF)
    return call(kernel, [like(left), part, part], 8, (), (far, left, right, low))


def plan(branch_shift):
    branches = branch_shift.shape[0]

    def kernel(shift_ref, out_ref):
        used = {}
        for d in INNER:
            hit = jnp.int32(0)
            for b in range(branches):
                hit = hit | (shift_ref[b] == d).astype(jnp.int32)
            used[d] = hit
        which = jnp.int32(0)
        for at, held in enumerate(SETS):
            same = jnp.int32(1)
            for d in INNER:
                same = same & (used[d] if d in held else 1 - used[d])
            which = which + same * at
        out_ref[0] = which

    return pl.pallas_call(
        kernel,
        out_shape=jax.ShapeDtypeStruct((1,), jnp.int32),
        in_specs=[SMEM],
        out_specs=SMEM,
        compiler_params=pltpu.CompilerParams(vmem_limit_bytes=GRANT),
    )(branch_shift)


def weights_of(branch_shift, gain):
    branches, size = gain.shape

    def kernel(shift_ref, gain_ref, *refs):
        *out_refs, done_ref, gain_t_ref = refs
        gain_t_ref[...] = gain_ref[...].T
        done_ref[...] = jnp.zeros_like(done_ref)
        energy, energies = lax.axis_index("energy"), lax.axis_size("energy")
        upper = lax.axis_index("slab") % 2 == 1
        first, last = jnp.int32(MAXS), jnp.int32(-MAXS)
        for b in range(branches):
            shift = shift_ref[b]
            inside = (shift > -MAXS) & (shift < MAXS)
            first = jnp.where(inside, jnp.minimum(first, shift), first)
            last = jnp.where(inside, jnp.maximum(last, shift), last)
        side = jnp.where(upper, -MAXS, MAXS)
        none = jnp.int32(10 * MAXS)
        distances = [side, -side, jnp.where(first < MAXS, first, none), jnp.where(last > first, last, none)]
        hits = []
        for distance in distances:
            inside = (energy + distance >= 0) & (energy + distance < energies)
            hits.append([
                jnp.where(inside & (shift_ref[b] == distance), 1.0, 0.0).astype(F32) for b in range(branches)
            ])

        @pl.loop(0, size // 64)
        def _(step):
            rows = pl.ds(pl.multiple_of(step * 64, 64), 64)
            outer = [gain_t_ref[rows, b : b + 1] * gain_ref[b : b + 1, :] for b in range(branches)]
            for out_ref, hit in zip(out_refs, hits):
                out_ref[rows, :] = sum(h * o for h, o in zip(hit, outer))

    out = jax.ShapeDtypeStruct((size, size), F32)
    return call(kernel, [out] * 4 + [DONE], 0, (branch_shift,), (gain,), [pltpu.VMEM((size, branches), F32)])


def combine(weights, mine, got_real, got_imag, *pieces):
    size = mine.shape[1]

    def kernel(*refs):
        weight_refs, (mine_ref, real_ref, imag_ref, *refs) = refs[: len(weights)], refs[len(weights) :]
        @pl.loop(0, size // 64)
        def _(step):
            rows = pl.ds(pl.multiple_of(step * 64, 64), 64)
            held = [weight_ref[rows, :] for weight_ref in weight_refs]
            for part, got_ref in enumerate((real_ref, imag_ref)):
                blocks = [mine_ref[part, rows, :], got_ref[rows, :]]
                blocks += [ref[part, rows, :] for ref in refs[:-1]]
                total = sum(w * block.astype(F32) for w, block in zip(held, blocks))
                refs[-1][part, rows, :] = total.astype(BF)

    return call(kernel, [like(mine)], 0, (), (*weights, mine, got_real, got_imag, *pieces))[0]


def local(inverses, coupling, slab_count, branch_shift, branch_gain):
    block = inverses[:, 0, 0]
    link = coupling[0]
    energies = lax.axis_size("energy")
    slabs = lax.axis_size("slab")
    lows, ups = range(0, slabs, 2), range(1, slabs, 2)

    def moved(value, slab_pairs, distance_of, reach=0):
        route = [
            (((e + distance_of(b)) % energies) * slabs + a, e * slabs + b)
            for e in range(energies)
            for a, b in slab_pairs
            if 0 <= e + reach < energies
        ]
        return lax.ppermute(value, BOTH, route)

    def side(b):
        return MAXS if b % 2 == 0 else -MAXS

    swap = [(i ^ 1, i) for i in range(slabs)]
    same = [(i, i) for i in range(slabs)]

    partner_block = lax.ppermute(block, "slab", swap)
    block, link = staged(block, link)
    left, right, both = own_slab(slab_count, block, link, partner_block)
    arrived = lax.ppermute(both, "slab", [(1, 3)])
    later_block, later_link, _ = tie((block, link, both))
    far = message(slab_count, later_block, partner_block)
    partner_link = lax.ppermute(later_link, "slab", swap)

    chip = chip_maps(slab_count, partner_block, partner_link, left, right)
    chip, arrived = tie((chip, arrived))
    green = sandwich(both, *chip, arrived)
    for k in range(3, slabs - 4, 2):
        further = lax.ppermute(green, "slab", [(k, k + 2)])
        if k == 3:
            far = moved(far, same, side)
        green = sandwich(both, *chip, arrived, further)

    to_upper = moved(green, [(b - 2, b) for b in ups if b > 1], side)
    to_lower = moved(green, [(b - 1, b) for b in lows if b > 0], side)

    far, shift, gain, _ = tie((far, branch_shift, branch_gain, green))
    *maps, maps_done = far_maps(far, link, partner_link)
    which = plan(shift)[0]
    *weights, weights_done = weights_of(shift, gain)
    to_upper, to_lower, which, _, _ = tie((to_upper, to_lower, which, maps_done, weights_done))

    low = far_low(far, maps[0], maps[1], to_upper, to_lower)
    mine, *give = far_up(far, maps[2], maps[3], low)

    def traded(give):
        return [lax.ppermute(part, "slab", swap) for part in give]

    def alone(weights, mine, *give):
        return combine(weights[:2], mine, *traded(give))

    def relayed(distances):
        def branch(weights, mine, *give):
            pieces = [moved(mine, same, lambda b, d=d: d - side(b), d) for d in distances]
            return combine(weights[: 2 + len(pieces)], mine, *traded(give), *pieces)

        return branch

    branches = [relayed(held) if held else alone for held in SETS]
    sigma = lax.switch(which, branches, weights, mine, *give)
    return sigma[:, None, None]


def solution(mesh):
    return jax.shard_map(
        local,
        mesh=mesh,
        in_specs=(
            P(None, "energy", "slab", None, None),
            P("slab", None, None),
            P("energy"),
            P(),
            P(),
        ),
        out_specs=P(None, "energy", "slab", None, None),
        check_vma=False,
    )
```

```python
import jax
import jax.numpy as jnp
from jax import lax
from jax.experimental import pallas as pl
from jax.experimental.pallas import tpu as pltpu
from jax.sharding import PartitionSpec as P

MAXS = 3
BF = jnp.bfloat16
F32 = jnp.float32
BOTH = ("energy", "slab")
ROWS = 512
EXTRA = 16
GRANT = 24 * 2**20
COST = 1024
tie = lax.optimization_barrier
VMEM = pl.BlockSpec(memory_space=pltpu.VMEM)
SMEM = pl.BlockSpec(memory_space=pltpu.SMEM)
DONE = jax.ShapeDtypeStruct((8, 128), F32)
INNER = list(range(1 - MAXS, MAXS))
SETS = [()] + [(d,) for d in INNER] + [(c, d) for i, c in enumerate(INNER) for d in INNER[i + 1 :]]


def dot(a, b):
    return jnp.dot(a, b, preferred_element_type=F32)


def call(kernel, outs, dots, scalars, arrays, scratch=()):
    return pl.pallas_call(
        kernel,
        out_shape=outs,
        in_specs=[SMEM] * len(scalars) + [VMEM] * len(arrays),
        out_specs=[VMEM] * len(outs),
        scratch_shapes=list(scratch),
        compiler_params=pltpu.CompilerParams(vmem_limit_bytes=GRANT),
        cost_estimate=pl.CostEstimate(
            flops=COST * dots, bytes_accessed=1024, transcendentals=0
        ),
    )(*scalars, *arrays)


def like(array):
    return jax.ShapeDtypeStruct(array.shape, array.dtype)


def steps(size, body):
    @pl.loop(0, size // ROWS)
    def _(step):
        body(pl.ds(pl.multiple_of(step * ROWS, ROWS), ROWS))


def put_maps(link_ref, block, on, left_ref, right_ref):
    def body(rows):
        for part in range(2):
            left = dot(block(part, rows), link_ref[...])
            left_ref[part, rows, :] = jnp.where(on, left, 0.0).astype(BF)
            right = lax.dot_general(
                link_ref[:, rows],
                block(part, slice(None)),
                (((0,), (0,)), ((), ())),
                preferred_element_type=F32,
            )
            right_ref[part, rows, :] = jnp.where(on, right, 0.0).astype(BF)

    steps(link_ref.shape[0], body)


def complex_rows(a_ref, rows, b_ref):
    ar, ai = a_ref[0, rows, :], a_ref[1, rows, :]
    return dot(ar, b_ref[0]) - dot(ai, b_ref[1]), dot(ar, b_ref[1]) + dot(ai, b_ref[0])


def put_sandwich(base, left_ref, right_ref, middle_ref, out_ref):
    def body(rows):
        hr, hi = complex_rows(left_ref, rows, middle_ref)
        hr, hi = hr.astype(BF), hi.astype(BF)
        rr, ri = right_ref[0], right_ref[1]
        parts[0][rows, :] = (base(0, rows).astype(F32) + dot(hr, rr) - dot(hi, ri)).astype(BF)
        parts[1][rows, :] = (base(1, rows).astype(F32) + dot(hr, ri) + dot(hi, rr)).astype(BF)

    parts = out_ref if isinstance(out_ref, tuple) else (out_ref.at[0], out_ref.at[1])
    steps(parts[0].shape[0], body)


def reader(ref, at=0):
    return lambda part, rows: ref[at + part, rows, :]


def staged(block, link):
    def kernel(block_ref, link_ref, block_out, link_out):
        block_out[...] = block_ref[...]
        link_out[...] = link_ref[...]

    return call(kernel, [like(block), like(link)], 0, (), (block, link))


def own_slab(slab_count, block, link, partner_block):
    def kernel(count_ref, block_ref, link_ref, partner_ref, left_ref, right_ref, both_ref):
        on = lax.axis_index("slab") < count_ref[0]
        put_maps(link_ref, reader(block_ref), on, left_ref, right_ref)
        put_sandwich(reader(block_ref), left_ref, right_ref, partner_ref, both_ref)

    return call(kernel, [like(block)] * 3, 12, (slab_count,), (block, link, partner_block))


def chip_maps(slab_count, partner_block, partner_link, left, right):
    def kernel(count_ref, block_ref, link_ref, l_ref, r_ref, left_ref, right_ref, ol_ref, or_ref):
        on = (lax.axis_index("slab") ^ 1) < count_ref[0]
        put_maps(link_ref, reader(block_ref), on, ol_ref, or_ref)

        def body(rows):
            for a_ref, b_ref, o_ref in ((l_ref, ol_ref, left_ref), (or_ref, r_ref, right_ref)):
                real, imag = complex_rows(a_ref, rows, b_ref)
                o_ref[0, rows, :] = real.astype(BF)
                o_ref[1, rows, :] = imag.astype(BF)

        steps(left.shape[1], body)

    scratch = [pltpu.VMEM(left.shape, BF)] * 2
    return call(kernel, [like(left)] * 2, 12, (slab_count,), (partner_block, partner_link, left, right), scratch)


def sandwich(base, left, right, *middles):
    def kernel(base_ref, left_ref, right_ref, *refs):
        middle_ref, out_ref = refs[0], refs[len(middles)]
        if len(middles) > 1:
            middle_ref = refs[-1]
            middle_ref[...] = refs[0][...] + refs[1][...]
        put_sandwich(reader(base_ref), left_ref, right_ref, middle_ref, out_ref)

    scratch = [pltpu.VMEM(base.shape, BF)] * (len(middles) > 1)
    return call(kernel, [like(base)], 8, (), (base, left, right, *middles), scratch)[0]


def message(slab_count, block, partner_block):
    size = block.shape[1]

    def kernel(count_ref, block_ref, partner_ref, out_ref):
        upper = lax.axis_index("slab") % 2 == 1
        low = jnp.where(upper, partner_ref[...], block_ref[...])
        high = jnp.where(upper, block_ref[...], partner_ref[...])
        for part in range(2):
            out_ref[pl.ds(part * size, size), :] = low[part]
            out_ref[pl.ds((2 + part) * size, size), :] = high[part]
        count = jnp.full((EXTRA, size), count_ref[0], jnp.int32).astype(F32)
        out_ref[pl.ds(4 * size, EXTRA), :] = count.astype(BF)

    out = jax.ShapeDtypeStruct((4 * size + EXTRA, size), BF)
    return call(kernel, [out], 0, (slab_count,), (block, partner_block))[0]


def far_block(far_ref, size, at):
    def read(part, rows):
        if isinstance(rows, slice):
            return far_ref[pl.ds((at + part) * size, size), :]
        return far_ref[pl.ds(pl.multiple_of((at + part) * size + rows.start, ROWS), ROWS), :]

    return read


def far_maps(far, link, partner_link):
    size = link.shape[0]

    def kernel(far_ref, link_ref, partner_ref, ll_ref, lr_ref, ul_ref, ur_ref, done_ref, held_ref):
        done_ref[...] = jnp.zeros_like(done_ref)
        position = lax.axis_index("slab")
        upper = position % 2 == 1
        low_at = ((position // 2) * 2).astype(F32)
        count = far_ref[pl.ds(4 * size, EXTRA), :].astype(F32)[:1]
        held_ref[...] = jnp.where(upper, partner_ref[...], link_ref[...])
        put_maps(held_ref, far_block(far_ref, size, 0), low_at < count, ll_ref, lr_ref)
        held_ref[...] = jnp.where(upper, link_ref[...], partner_ref[...])
        put_maps(held_ref, far_block(far_ref, size, 2), low_at + 1 < count, ul_ref, ur_ref)

    maps = jax.ShapeDtypeStruct((2, size, size), BF)
    return call(kernel, [maps] * 4 + [DONE], 8, (), (far, link, partner_link), [pltpu.VMEM(link.shape, BF)])


def far_low(far, left, right, first, second):
    size = left.shape[-1]

    def kernel(far_ref, left_ref, right_ref, a_ref, b_ref, out_ref, middle_ref):
        middle_ref[...] = a_ref[...] + b_ref[...]
        put_sandwich(far_block(far_ref, size, 0), left_ref, right_ref, middle_ref, out_ref)

    return call(kernel, [like(left)], 8, (), (far, left, right, first, second), [pltpu.VMEM(left.shape, BF)])[0]


def far_up(far, left, right, low):
    size = left.shape[-1]

    def kernel(far_ref, left_ref, right_ref, low_ref, mine_ref, *give_refs):
        upper = lax.axis_index("slab") % 2 == 1

        @pl.when(upper)
        def _():
            put_sandwich(far_block(far_ref, size, 2), left_ref, right_ref, low_ref, mine_ref)
            for part in range(2):
                give_refs[part][...] = low_ref[part]

        @pl.when(jnp.logical_not(upper))
        def _():
            put_sandwich(far_block(far_ref, size, 2), left_ref, right_ref, low_ref, give_refs)
            mine_ref[...] = low_ref[...]

    part = jax.ShapeDtypeStruct((size, size), BF)
    return call(kernel, [like(left), part, part], 8, (), (far, left, right, low))


def plan(branch_shift):
    branches = branch_shift.shape[0]

    def kernel(shift_ref, out_ref):
        used = {}
        for d in INNER:
            hit = jnp.int32(0)
            for b in range(branches):
                hit = hit | (shift_ref[b] == d).astype(jnp.int32)
            used[d] = hit
        which = jnp.int32(0)
        for at, held in enumerate(SETS):
            same = jnp.int32(1)
            for d in INNER:
                same = same & (used[d] if d in held else 1 - used[d])
            which = which + same * at
        out_ref[0] = which

    return pl.pallas_call(
        kernel,
        out_shape=jax.ShapeDtypeStruct((1,), jnp.int32),
        in_specs=[SMEM],
        out_specs=SMEM,
        compiler_params=pltpu.CompilerParams(vmem_limit_bytes=GRANT),
    )(branch_shift)


def weights_of(branch_shift, gain):
    branches, size = gain.shape

    def kernel(shift_ref, gain_ref, *refs):
        *out_refs, done_ref, gain_t_ref = refs
        gain_t_ref[...] = gain_ref[...].T
        done_ref[...] = jnp.zeros_like(done_ref)
        energy, energies = lax.axis_index("energy"), lax.axis_size("energy")
        upper = lax.axis_index("slab") % 2 == 1
        first, last = jnp.int32(MAXS), jnp.int32(-MAXS)
        for b in range(branches):
            shift = shift_ref[b]
            inside = (shift > -MAXS) & (shift < MAXS)
            first = jnp.where(inside, jnp.minimum(first, shift), first)
            last = jnp.where(inside, jnp.maximum(last, shift), last)
        side = jnp.where(upper, -MAXS, MAXS)
        none = jnp.int32(10 * MAXS)
        distances = [side, -side, jnp.where(first < MAXS, first, none), jnp.where(last > first, last, none)]
        hits = []
        for distance in distances:
            inside = (energy + distance >= 0) & (energy + distance < energies)
            hits.append([
                jnp.where(inside & (shift_ref[b] == distance), 1.0, 0.0).astype(F32) for b in range(branches)
            ])

        @pl.loop(0, size // 32)
        def _(step):
            rows = pl.ds(pl.multiple_of(step * 32, 32), 32)
            outer = [gain_t_ref[rows, b : b + 1] * gain_ref[b : b + 1, :] for b in range(branches)]
            for out_ref, hit in zip(out_refs, hits):
                out_ref[rows, :] = sum(h * o for h, o in zip(hit, outer))

    out = jax.ShapeDtypeStruct((size, size), F32)
    return call(kernel, [out] * 4 + [DONE], 0, (branch_shift,), (gain,), [pltpu.VMEM((size, branches), F32)])


def combine(weights, mine, got_real, got_imag, *pieces):
    size = mine.shape[1]

    def kernel(*refs):
        weight_refs, (mine_ref, real_ref, imag_ref, *refs) = refs[: len(weights)], refs[len(weights) :]
        @pl.loop(0, size // 32)
        def _(step):
            rows = pl.ds(pl.multiple_of(step * 32, 32), 32)
            held = [weight_ref[rows, :] for weight_ref in weight_refs]
            for part, got_ref in enumerate((real_ref, imag_ref)):
                blocks = [mine_ref[part, rows, :], got_ref[rows, :]]
                blocks += [ref[part, rows, :] for ref in refs[:-1]]
                total = sum(w * block.astype(F32) for w, block in zip(held, blocks))
                refs[-1][part, rows, :] = total.astype(BF)

    return call(kernel, [like(mine)], 0, (), (*weights, mine, got_real, got_imag, *pieces))[0]


def local(inverses, coupling, slab_count, branch_shift, branch_gain):
    block = inverses[:, 0, 0]
    link = coupling[0]
    energies = lax.axis_size("energy")
    slabs = lax.axis_size("slab")
    lows, ups = range(0, slabs, 2), range(1, slabs, 2)

    def moved(value, slab_pairs, distance_of, reach=0):
        route = [
            (((e + distance_of(b)) % energies) * slabs + a, e * slabs + b)
            for e in range(energies)
            for a, b in slab_pairs
            if 0 <= e + reach < energies
        ]
        return lax.ppermute(value, BOTH, route)

    def side(b):
        return MAXS if b % 2 == 0 else -MAXS

    swap = [(i ^ 1, i) for i in range(slabs)]
    same = [(i, i) for i in range(slabs)]

    partner_block = lax.ppermute(block, "slab", swap)
    block, link = staged(block, link)
    left, right, both = own_slab(slab_count, block, link, partner_block)
    arrived = lax.ppermute(both, "slab", [(1, 3)])
    later_block, later_link, _ = tie((block, link, both))
    far = message(slab_count, later_block, partner_block)
    partner_link = lax.ppermute(later_link, "slab", swap)

    chip = chip_maps(slab_count, partner_block, partner_link, left, right)
    chip, arrived = tie((chip, arrived))
    green = sandwich(both, *chip, arrived)
    for k in range(3, slabs - 4, 2):
        further = lax.ppermute(green, "slab", [(k, k + 2)])
        if k == 3:
            far = moved(far, same, side)
        green = sandwich(both, *chip, arrived, further)

    to_upper = moved(green, [(b - 2, b) for b in ups if b > 1], side)
    to_lower = moved(green, [(b - 1, b) for b in lows if b > 0], side)

    far, shift, gain, _ = tie((far, branch_shift, branch_gain, green))
    *maps, maps_done = far_maps(far, link, partner_link)
    which = plan(shift)[0]
    *weights, weights_done = weights_of(shift, gain)
    to_upper, to_lower, which, _, _ = tie((to_upper, to_lower, which, maps_done, weights_done))

    low = far_low(far, maps[0], maps[1], to_upper, to_lower)
    mine, *give = far_up(far, maps[2], maps[3], low)

    def traded(give):
        return [lax.ppermute(part, "slab", swap) for part in give]

    def alone(weights, mine, *give):
        return combine(weights[:2], mine, *traded(give))

    def relayed(distances):
        def branch(weights, mine, *give):
            pieces = [moved(mine, same, lambda b, d=d: d - side(b), d) for d in distances]
            return combine(weights[: 2 + len(pieces)], mine, *traded(give), *pieces)

        return branch

    branches = [relayed(held) if held else alone for held in SETS]
    sigma = lax.switch(which, branches, weights, mine, *give)
    return sigma[:, None, None]


def solution(mesh):
    return jax.shard_map(
        local,
        mesh=mesh,
        in_specs=(
            P(None, "energy", "slab", None, None),
            P("slab", None, None),
            P("energy"),
            P(),
            P(),
        ),
        out_specs=P(None, "energy", "slab", None, None),
        check_vma=False,
    )
```
